256 devices in a mesh: slab: 16 (over y, z_lo), chan: 16 (over z_hi, x, core).
Axes of the slice: x: 4, y: 4, z: 8 (z_hi: 2, z_lo: 4; z = z_hi * 4 + z_lo), core: 2. Of those that a mesh axis runs over, the one named last changes fastest.
Arguments:
- saved_input: float32 [512, 96, 256], P('chan', 'slab'), may hold values from -6 to 6
- pre_first: float32 [512, 96, 256], P('chan', 'slab'), may hold values from -8 to 8
- pre_second: float32 [512, 96, 256], P('chan', 'slab'), may hold values from -8 to 8
- out_grad: float32 [512, 96, 256], P('chan', 'slab'), may hold values from -12 to 12
- weight_first: float32 [27, 512, 512], P(None, 'chan'), may hold values from -0.0546875 to 0.0546875
- weight_second: float32 [27, 512, 512], P(None, 'chan'), may hold values from -0.0546875 to 0.0546875
Outputs:
- input_grad: float32 [512, 96, 256], P('chan', 'slab')
- grad_weight_first: float32 [27, 512, 512], P(None, 'chan', 'slab')
- grad_weight_second: float32 [27, 512, 512], P(None, 'chan', 'slab')
The draws below stay inside these ranges and needn't reach their ends.
All inputs are finite; a program needn't handle non-finite values.
Results may differ from the reference program's by a relative error of at most 0.00013.
Values sent between devices are 32-bit elements; how exact they have to be, the bound alone decides.
No kernel may reach another device: no remote copies, remote signals or barrier semaphores. Data moves between devices by JAX's collectives and lax.ppermute only.
A program may use at most 128 MiB of HBM per device.

```python
import math
import jax
import jax.numpy as jnp
from jax import lax

C = 512
TAPS = 27
AREA = 256
PLANES = 96


def with_spikes(result, stream_key, source, target, blocks, factor):
    def block_of(axis_at):
        return (jnp.arange(result.shape[axis_at]) // (result.shape[axis_at] // blocks)).reshape((-1,) + (1,) * (result.ndim - 1 - axis_at))

    first = jax.random.permutation(stream_key, blocks)[block_of(target)]
    other_side = (block_of(target) + blocks // 2) % blocks
    return jnp.where((block_of(source) == first) | (block_of(source) == other_side), factor * result, result)


def block_scale(own_key, dims, shards, least, high):
    level = 1.0
    for position, blocks in shards:
        steps = jax.random.uniform(jax.random.fold_in(jax.random.fold_in(own_key, 6), position), (blocks,), jnp.float32, least / len(shards), high / len(shards))
        level = level * jnp.repeat(jnp.exp(steps), dims[position] // blocks).reshape((-1,) + (1,) * (len(dims) - 1 - position))
    return level


def scatter_about(rng, shape, scale, limit, split=(), kind=jnp.bfloat16):
    gain = block_scale(rng, shape, split, -0.22, 0.18) if split else 1.0
    array = jax.random.normal(rng, shape, jnp.float32) * scale * gain
    return jnp.minimum(jnp.maximum(array, -limit), limit).astype(kind)


def gaussian_with(stream_key, shape, width, reach, shards, heavy, dtype=jnp.bfloat16):
    drawn = width * jax.random.normal(stream_key, shape, jnp.float32)
    if shards:
        drawn = drawn * block_scale(stream_key, shape, shards, -0.22, 0.18)
    return jnp.clip(with_spikes(drawn, jax.random.fold_in(stream_key, 3), *heavy), -reach, reach).astype(dtype)


def setup_inputs(seed: int = 0) -> dict:
    splits = jax.random.split(jax.random.key(seed), 7)
    saved_input = scatter_about(splits[0], (C, PLANES, AREA), 1.0, 6.0, ((0, 16), (1, 16)), jnp.float32)
    pre_first = scatter_about(splits[1], (C, PLANES, AREA), 1.5, 8.0, ((0, 16), (1, 16)), jnp.float32)
    pre_second = scatter_about(splits[2], (C, PLANES, AREA), 1.5, 8.0, ((0, 16), (1, 16)), jnp.float32)
    out_grad = gaussian_with(splits[3], (C, PLANES, AREA), 2.0, 12.0, ((0, 16), (1, 16)), (1, 0, 16, 2.0), jnp.float32)
    weight_first = scatter_about(splits[4], (TAPS, C, C), (27 * C) ** -0.5, 0.0546875, ((1, 16),), jnp.float32)
    weight_second = scatter_about(splits[5], (TAPS, C, C), (27 * C) ** -0.5, 0.0546875, ((1, 16),), jnp.float32)
    return {"saved_input": saved_input, "pre_first": pre_first, "pre_second": pre_second, "out_grad": out_grad, "weight_first": weight_first, "weight_second": weight_second}


OFFSETS = [(depth_step, row_step, col_step) for depth_step in (-1, 0, 1) for row_step in (-1, 0, 1) for col_step in (-1, 0, 1)]

def silu_slope(values):
    sigma = jax.nn.sigmoid(values)
    return sigma * (1.0 + values * (1.0 - sigma))

def layer_back(layer_input, grad_out, weight):
    channels, planes, area_cells = layer_input.shape
    side_len = math.isqrt(area_cells)
    widths = ((0, 0), (1, 1), (1, 1), (1, 1))
    input_pad = jnp.pad(layer_input.reshape(channels, planes, side_len, side_len), widths)
    grad_pad = jnp.pad(grad_out.reshape(channels, planes, side_len, side_len), widths)
    grad_flat = grad_out.reshape(channels, planes * area_cells)
    grad_in = jnp.zeros((channels, planes * area_cells), jnp.float32)
    weight_rows = []
    for tap_index, (depth_step, row_step, col_step) in enumerate(OFFSETS):
        grad_shift = grad_pad[:, 1 - depth_step:1 - depth_step + planes, 1 - row_step:1 - row_step + side_len, 1 - col_step:1 - col_step + side_len]
        grad_in = grad_in + jnp.dot(weight[tap_index], grad_shift.reshape(channels, -1), precision=lax.Precision.HIGHEST, preferred_element_type=jnp.float32)
        input_shift = input_pad[:, 1 + depth_step:1 + depth_step + planes, 1 + row_step:1 + row_step + side_len, 1 + col_step:1 + col_step + side_len]
        weight_rows.append(lax.dot_general(input_shift.reshape(channels, -1), grad_flat, (((1,), (1,)), ((), ())), precision=lax.Precision.HIGHEST, preferred_element_type=jnp.float32))
    grad_weight = jnp.stack(weight_rows, 0) / math.sqrt(planes * area_cells)
    return (grad_in.reshape(channels, planes, area_cells), grad_weight)

def reference(saved_input, pre_first, pre_second, out_grad, weight_first, weight_second):
    hidden = jax.nn.silu(pre_first)
    second_grad = out_grad * silu_slope(pre_second)
    hidden_grad, grad_weight_second = layer_back(hidden, second_grad, weight_second)
    first_grad = hidden_grad * silu_slope(pre_first)
    input_grad, grad_weight_first = layer_back(saved_input, first_grad, weight_first)
    return (input_grad, grad_weight_first, grad_weight_second)
```

```python
import math

import jax
import jax.numpy as jnp
from jax import lax
from jax.experimental import pallas as pl
from jax.experimental.pallas import tpu as pltpu
from jax.sharding import PartitionSpec as P

SIDE = 16
AREA = 256
SLABS = 16
SHIFTS = [(b, c) for b in (-1, 0, 1) for c in (-1, 0, 1)]
F32 = jnp.float32
BF16 = jnp.bfloat16
VM = pl.BlockSpec(memory_space=pltpu.VMEM)
SM = pl.BlockSpec(memory_space=pltpu.SMEM)


def slope_of(values):
    sigma = jax.nn.sigmoid(values)
    return sigma * (1.0 + values * (1.0 - sigma))


def call(kernel, out_shape, scratch, args, n_smem=0, flops=0, name=None):
    many = isinstance(out_shape, list)
    moved = sum(a.size * a.dtype.itemsize for a in args)
    moved += sum(o.size * o.dtype.itemsize for o in (out_shape if many else [out_shape]))
    return pl.pallas_call(
        kernel,
        out_shape=out_shape,
        in_specs=[SM] * n_smem + [VM] * (len(args) - n_smem),
        out_specs=[VM] * len(out_shape) if many else VM,
        scratch_shapes=scratch,
        compiler_params=pltpu.CompilerParams(vmem_limit_bytes=40 << 20),
        cost_estimate=pl.CostEstimate(flops=flops, bytes_accessed=moved, transcendentals=0),
        name=name,
    )(*args)


def shape(*dims, dtype=F32):
    return jax.ShapeDtypeStruct(dims, dtype)


def split(value):
    high = value.astype(BF16)
    return high, (value - high.astype(F32)).astype(BF16)


def moved_cells(plane, row_step, col_step):
    cells = lax.broadcasted_iota(jnp.int32, plane.shape, 1)
    if col_step:
        col = cells % SIDE + col_step
        plane = jnp.where((col >= 0) & (col < SIDE), pltpu.roll(plane, -col_step % AREA, 1), 0.0)
    if row_step:
        row = cells // SIDE + row_step
        plane = jnp.where((row >= 0) & (row < SIDE), pltpu.roll(plane, -row_step * SIDE % AREA, 1), 0.0)
    return plane


def scaled_kernel(pre_ref, grad_ref, out_ref):
    for p in range(out_ref.shape[0]):
        out_ref[p] = grad_ref[:, p, :] * slope_of(pre_ref[:, p, :])


def scaled(pre, grad):
    channels, planes, area = pre.shape
    return call(scaled_kernel, shape(planes, channels, area), [], [pre, grad], name="scaled")


def prepare_kernel(pre_ref, saved_ref, low_ref, high_ref, w1_ref, w2_ref,
                   h_hi, h_lo, x_hi, x_lo, w1_hi, w1_lo, w2_hi, w2_lo, slope_ref, rows):
    planes = slope_ref.shape[0]
    channels = slope_ref.shape[1]
    for n, (own, hi_ref, lo_ref) in enumerate(((pre_ref, h_hi, h_lo), (saved_ref, x_hi, x_lo))):
        rows[0] = low_ref[n]
        rows[planes + 1] = high_ref[n]
        for p in range(planes):
            rows[p + 1] = own[:, p, :]
            if n == 0:
                slope_ref[p] = slope_of(own[:, p, :])

        def one_plane(q, _):
            plane = rows[q]
            if n == 0:
                plane = plane * jax.nn.sigmoid(plane)
            lanes = pl.ds(pl.multiple_of(q * AREA, AREA), AREA)
            for s, (b, c) in enumerate(SHIFTS):
                hi, lo = split(moved_cells(plane, b, c))
                hi_ref[s * channels:(s + 1) * channels, lanes] = hi
                lo_ref[s * channels:(s + 1) * channels, lanes] = lo
            return 0

        lax.fori_loop(0, planes + 2, one_plane, 0)
    for source, hi_ref, lo_ref in ((w2_ref, w2_hi, w2_lo), (w1_ref, w1_hi, w1_lo)):

        def one_tap(t, _):
            at = pl.ds(pl.multiple_of(t * channels, channels), channels)
            hi, lo = split(source[t])
            hi_ref[at, :] = hi
            lo_ref[at, :] = lo
            return 0

        lax.fori_loop(0, source.shape[0], one_tap, 0)


def prepared(pre, saved, low, high, w1, w2):
    channels, planes, area = pre.shape
    taps, _, total = w1.shape
    tall = shape(len(SHIFTS) * channels, (planes + 2) * area, dtype=BF16)
    flat = shape(taps * channels, total, dtype=BF16)
    outs = [tall] * 4 + [flat] * 4 + [shape(planes, channels, area)]
    return call(prepare_kernel, outs, [pltpu.VMEM((planes + 2, channels, area), F32)],
                [pre, saved, low, high, w1, w2], name="prepared")


def gather_blocks(spots, pieces, g_hi, g_lo):
    planes = pieces[0].shape[0]
    for k, piece in enumerate(pieces):
        spot = spots[k]

        def one(p, _):
            lanes = pl.ds(pl.multiple_of(p * AREA, AREA), AREA)
            hi, lo = split(piece[p])
            g_hi[spot, :, lanes] = hi
            g_lo[spot, :, lanes] = lo
            return 0

        lax.fori_loop(0, planes, one, 0, unroll=True)


def data_kernel(n_pieces, spots, *refs):
    pieces, (w_hi, w_lo, own_ref, before_ref, after_ref, g_hi, g_lo, sums) = refs[:n_pieces], refs[n_pieces:]
    planes, channels, _ = own_ref.shape
    total = w_hi.shape[1]
    third = len(SHIFTS) * channels
    gather_blocks(spots, pieces, g_hi, g_lo)
    sums[...] = jnp.zeros_like(sums)

    def one_plane(p, _):
        lanes = pl.ds(pl.multiple_of(p * AREA, AREA), AREA)
        hi = g_hi[:, :, lanes].reshape(total, AREA)
        lo = g_lo[:, :, lanes].reshape(total, AREA)
        for a in range(3):
            w_a = w_hi[a * third:(a + 1) * third, :]
            out = jnp.dot(w_a, hi, preferred_element_type=F32)
            out += jnp.dot(w_a, lo, preferred_element_type=F32)
            out += jnp.dot(w_lo[a * third:(a + 1) * third, :], hi, preferred_element_type=F32)
            sums[p + a] += out
        return 0

    lax.fori_loop(0, planes, one_plane, 0)

    def spread(q):
        total_plane = jnp.zeros((channels, AREA), F32)
        for b in (-1, 0, 1):
            row = jnp.zeros((channels, AREA), F32)
            for c in (-1, 0, 1):
                s = SHIFTS.index((b, c)) * channels
                row += moved_cells(sums[q, s:s + channels, :], 0, -c)
            total_plane += moved_cells(row, -b, 0)
        return total_plane

    before_ref[...] = spread(0)
    after_ref[...] = spread(planes + 1)

    def one_out(p, _):
        own_ref[p] = spread(p + 1)
        return 0

    lax.fori_loop(0, planes, one_out, 0)


def data_gradient(spots, pieces, w_hi, w_lo):
    planes, channels, area = pieces[0].shape
    rows, total = w_hi.shape
    blocks = total // channels
    kernel = lambda *refs: data_kernel(len(pieces), *refs)
    outs = [shape(planes, channels, area), shape(channels, area), shape(channels, area)]
    scratch = [pltpu.VMEM((blocks, channels, planes * area), BF16)] * 2
    scratch += [pltpu.VMEM((planes + 2, rows // 3, area), F32)]
    return call(kernel, outs, scratch, [spots, *pieces, w_hi, w_lo], 1, 6 * rows * total * planes * area,
                name="data_gradient")


def filter_kernel(n_pieces, spots, *refs):
    pieces, (i_hi, i_lo), outs, (g_hi, g_lo) = (
        refs[:n_pieces], refs[n_pieces:n_pieces + 2], refs[n_pieces + 2:-2], refs[-2:])
    planes = pieces[0].shape[0]
    total = g_hi.shape[0] * g_hi.shape[1]
    width = total // len(outs)
    gather_blocks(spots, pieces, g_hi, g_lo)
    for out in outs:
        out[...] = jnp.zeros_like(out)

    def one_plane(p, _):
        lanes = pl.ds(pl.multiple_of(p * AREA, AREA), AREA)
        hi = g_hi[:, :, lanes].reshape(total, AREA)
        lo = g_lo[:, :, lanes].reshape(total, AREA)
        windows = [pl.ds(pl.multiple_of((p + a) * AREA, AREA), AREA) for a in range(3)]
        left_hi = jnp.concatenate([i_hi[:, w] for w in windows], 0)
        left_lo = jnp.concatenate([i_lo[:, w] for w in windows], 0)
        dims = (((1,), (1,)), ((), ()))
        part = lax.dot_general(left_hi, hi, dims, preferred_element_type=F32)
        part += lax.dot_general(left_hi, lo, dims, preferred_element_type=F32)
        part += lax.dot_general(left_lo, hi, dims, preferred_element_type=F32)
        for d, out in enumerate(outs):
            out[...] += part[:, d * width:(d + 1) * width]
        return 0

    lax.fori_loop(0, planes, one_plane, 0)


def filter_gradient(spots, pieces, i_hi, i_lo, parts):
    planes, channels, area = pieces[0].shape
    rows = 3 * i_hi.shape[0]
    total = channels * len(pieces)
    kernel = lambda *refs: filter_kernel(len(pieces), *refs)
    outs = [shape(rows, total // parts)] * parts
    scratch = [pltpu.VMEM((len(pieces), channels, planes * area), BF16)] * 2
    return call(kernel, outs, scratch, [spots, *pieces, i_hi, i_lo], 1, 6 * rows * total * planes * area,
                name="filter_gradient")


def turned_kernel(spots, a, b, c, d, *refs):
    outs, turned = refs[:-1], refs[-1]
    turned[...] = (a[...] + b[...] + c[...] + d[...]).T
    height = outs[0].shape[0]
    for k, out in enumerate(outs):
        out[...] = turned[pl.ds(pl.multiple_of(spots[k] * height, height), height), :]


def turned_sum(spots, parts):
    rows, width = parts[0].shape
    return call(turned_kernel, [shape(width // 4, rows)] * 4, [pltpu.VMEM((width, rows), F32)],
                [spots, *parts], 1, name="turned_sum")


def last_kernel(scale, a, b, c, d, out):
    out[...] = ((a[...] + b[...] + c[...] + d[...]) * scale).T


def last_sum(parts, scale):
    height, rows = parts[0].shape
    return call(lambda *refs: last_kernel(scale, *refs), shape(rows, height), [], parts, name="last_sum")


def first_kernel(own, before, after, slope, out):
    planes = out.shape[0]
    for p in range(planes):
        value = own[p]
        if p == 0:
            value = value + before[...]
        if p == planes - 1:
            value = value + after[...]
        out[p] = value * slope[p]


def input_kernel(own, before, after, out):
    planes = own.shape[0]
    for p in range(planes):
        value = own[p]
        if p == 0:
            value = value + before[...]
        if p == planes - 1:
            value = value + after[...]
        out[:, p, :] = value


FAR = [(i, (i + 8) % 16) for i in range(16)]
TWIN = [(i, i ^ 1) for i in range(16)]
UP = [(i, i + 1) for i in range(SLABS - 1)]
DOWN = [(i + 1, i) for i in range(SLABS - 1)]


def along_x(d):
    return [(i, (i & 9) | ((i + 2 * d) & 6)) for i in range(16)]


def along_y(d):
    return [(i, (i + 4 * d) % 16) for i in range(16)]


def along_z(d):
    return [(i, (i & 12) | ((i + d) & 3)) for i in range(16)]


def send(value, moves, axis="chan"):
    return lax.ppermute(value, axis, moves)


def gathered(own):
    me = lax.axis_index("chan")
    far = send(own, FAR)
    pieces, ids = [own, far], [me, me ^ 8]
    for value, shard in ((own, me), (far, me ^ 8)):
        for d in (1, 3, 2):
            pieces.append(send(value, along_x(d)))
            ids.append((shard & 9) | ((shard - 2 * d) & 6))
    pieces += [send(piece, TWIN) for piece in pieces]
    ids += [shard ^ 1 for shard in ids]
    return pieces, jnp.stack(ids).astype(jnp.int32)


def edges(before, after):
    return send(after, UP, "slab"), send(before, DOWN, "slab")


def owner_sum(parts, spots, scale):
    arrived = [parts[0]] + [send(parts[d], along_y(d), "slab") for d in (2, 1, 3)]
    rows = turned_sum(spots, arrived)
    arrived = [rows[0]] + [send(rows[d], along_z(d), "slab") for d in (1, 2, 3)]
    return last_sum(arrived, scale)


def per_device(saved_input, pre_first, pre_second, out_grad, weight_first, weight_second):
    channels, planes, area = saved_input.shape
    taps, _, total = weight_first.shape
    scale = 1.0 / math.sqrt(planes * SLABS * area)
    slab = lax.axis_index("slab")
    y_spot = slab // 4
    z_spots = ((slab + jnp.arange(4)) % 4).astype(jnp.int32)

    second_grad = scaled(pre_second, out_grad)
    pieces, ids = gathered(second_grad)
    quarters = (((ids // 4 - y_spot) % 4) * 4 + ids % 4).astype(jnp.int32)

    low = send(jnp.stack([pre_first[:, planes - 1], saved_input[:, planes - 1]]), UP, "slab")
    high = send(jnp.stack([pre_first[:, 0], saved_input[:, 0]]), DOWN, "slab")
    h_hi, h_lo, x_hi, x_lo, w1_hi, w1_lo, w2_hi, w2_lo, slope = prepared(
        pre_first, saved_input, low, high, weight_first, weight_second)

    own, before, after = data_gradient(ids, pieces, w2_hi, w2_lo)
    first_grad = call(first_kernel, shape(planes, channels, area), [],
                      [own, *edges(before, after), slope], name="first_grad")
    second_parts = filter_gradient(quarters, pieces, h_hi, h_lo, 4)

    pieces, ids = gathered(first_grad)
    second_weights = owner_sum(second_parts, z_spots, scale)
    first_parts = filter_gradient(quarters, pieces, x_hi, x_lo, 4)
    first_weights = owner_sum(first_parts, z_spots, scale)
    own, before, after = data_gradient(ids, pieces, w1_hi, w1_lo)
    input_grad = call(input_kernel, shape(channels, planes, area), [], [own, *edges(before, after)], name="input_grad")
    return (input_grad, first_weights.reshape(taps, channels, -1), second_weights.reshape(taps, channels, -1))


def solution(mesh):
    in_specs = (
        P("chan", "slab", None),
        P("chan", "slab", None),
        P("chan", "slab", None),
        P("chan", "slab", None),
        P(None, "chan", None),
        P(None, "chan", None),
    )
    out_specs = (P("chan", "slab", None), P(None, "chan", "slab"), P(None, "chan", "slab"))
    return jax.shard_map(
        per_device, mesh=mesh, in_specs=in_specs, out_specs=out_specs, check_vma=False
    )
```

```python
import math

import jax
import jax.numpy as jnp
from jax import lax
from jax.experimental import pallas as pl
from jax.experimental.pallas import tpu as pltpu
from jax.sharding import PartitionSpec as P

SIDE = 16
AREA = 256
SLABS = 16
SHIFTS = [(b, c) for b in (-1, 0, 1) for c in (-1, 0, 1)]
F32 = jnp.float32
BF16 = jnp.bfloat16
VM = pl.BlockSpec(memory_space=pltpu.VMEM)
SM = pl.BlockSpec(memory_space=pltpu.SMEM)


def slope_of(values):
    sigma = jax.nn.sigmoid(values)
    return sigma * (1.0 + values * (1.0 - sigma))


def call(kernel, out_shape, scratch, args, n_smem=0, flops=0, name=None, fetched=()):
    many = isinstance(out_shape, list)
    moved = sum(a.size * a.dtype.itemsize for a in (*args, *fetched))
    moved += sum(o.size * o.dtype.itemsize for o in (out_shape if many else [out_shape]))
    n, m = len(args), len(fetched)

    def whole(*refs):
        sources, rest = refs[n:n + m], refs[n + m:]
        rest, targets, sems = rest[:len(rest) - m - 1], rest[len(rest) - m - 1:-1], rest[-1]
        copies = [(pltpu.make_async_copy(s, t, sems.at[k]), t) for k, (s, t) in enumerate(zip(sources, targets))]
        for copy, _ in copies:
            copy.start()
        kernel(copies, *refs[:n], *rest)

    if fetched:
        scratch = [*scratch, *(pltpu.VMEM(f.shape, f.dtype) for f in fetched), pltpu.SemaphoreType.DMA((m,))]
    return pl.pallas_call(
        whole if fetched else kernel,
        out_shape=out_shape,
        in_specs=[SM] * n_smem + [VM] * (n - n_smem) + [pl.BlockSpec(memory_space=pltpu.HBM)] * m,
        out_specs=[VM] * len(out_shape) if many else VM,
        scratch_shapes=scratch,
        compiler_params=pltpu.CompilerParams(vmem_limit_bytes=16 << 20),
        cost_estimate=pl.CostEstimate(flops=flops, bytes_accessed=moved, transcendentals=0),
        name=name,
    )(*args, *fetched)


def arrived(copies):
    for copy, _ in copies:
        copy.wait()
    return [target for _, target in copies]


def shape(*dims, dtype=F32):
    return jax.ShapeDtypeStruct(dims, dtype)


def split(value):
    high = value.astype(BF16)
    return high, (value - high.astype(F32)).astype(BF16)


def moved_cells(plane, row_step, col_step):
    cells = lax.broadcasted_iota(jnp.int32, plane.shape, 1)
    if col_step:
        col = cells % SIDE + col_step
        plane = jnp.where((col >= 0) & (col < SIDE), pltpu.roll(plane, -col_step % AREA, 1), 0.0)
    if row_step:
        row = cells // SIDE + row_step
        plane = jnp.where((row >= 0) & (row < SIDE), pltpu.roll(plane, -row_step * SIDE % AREA, 1), 0.0)
    return plane


def scaled_kernel(pre_ref, grad_ref, out_ref):
    out_ref[...] = grad_ref[...] * slope_of(pre_ref[...])


def scaled(pre, grad):
    return call(scaled_kernel, shape(*pre.shape), [], [pre, grad], name="scaled")


def weights_kernel(copies, turn, pre_ref, *outs):
    slope_ref = outs[-1]
    slope_ref[...] = slope_of(pre_ref[...])
    for n, copy in enumerate(copies):
        source, = arrived([copy])
        taps, channels, total = source.shape
        width = total // 4
        for a in range(3):
            hi_ref, lo_ref = outs[6 * n + 2 * a:6 * n + 2 * a + 2]

            def one_tap(t, _):
                at = pl.ds(pl.multiple_of(t * channels, channels), channels)
                for d in range(4):
                    lanes = pl.ds(pl.multiple_of(turn[d] * width, width), width)
                    hi, lo = split(source[t + a * (taps // 3), :, lanes])
                    hi_ref[at, d * width:(d + 1) * width] = hi
                    lo_ref[at, d * width:(d + 1) * width] = lo
                return 0

            lax.fori_loop(0, taps // 3, one_tap, 0)


def weight_halves(turn, pre, w1, w2):
    taps, channels, total = w1.shape
    flat = shape(taps // 3 * channels, total, dtype=BF16)
    *halves, slope = call(weights_kernel, [flat] * 12 + [shape(*pre.shape)], [], [turn, pre], 1,
                          name="weight_halves", fetched=[w2, w1])
    return halves[:6], halves[6:], slope


def inputs_kernel(pre_ref, saved_ref, low_ref, high_ref, h_hi, h_lo, x_hi, x_lo, rows):
    planes, channels, _ = pre_ref.shape
    for n, (own, hi_ref, lo_ref) in enumerate(((pre_ref, h_hi, h_lo), (saved_ref, x_hi, x_lo))):
        rows[0] = low_ref[n + 1]
        rows[planes + 1] = high_ref[n + 1]
        rows[1:planes + 1] = own[...]

        def one_plane(q, _):
            plane = rows[q]
            if n == 0:
                plane = plane * jax.nn.sigmoid(plane)
            lanes = pl.ds(pl.multiple_of(q * AREA, AREA), AREA)
            for s, (b, c) in enumerate(SHIFTS):
                hi, lo = split(moved_cells(plane, b, c))
                hi_ref[s * channels:(s + 1) * channels, lanes] = hi
                lo_ref[s * channels:(s + 1) * channels, lanes] = lo
            return 0

        lax.fori_loop(0, planes + 2, one_plane, 0)


def input_halves(pre, saved, low, high):
    planes, channels, area = pre.shape
    tall = shape(len(SHIFTS) * channels, (planes + 2) * area, dtype=BF16)
    return call(inputs_kernel, [tall] * 4, [pltpu.VMEM((planes + 2, channels, area), F32)],
                [pre, saved, low, high], name="input_halves")


def gather_blocks(spots, pieces, g_hi, g_lo):
    planes = pieces[0].shape[0]
    k = 0
    for piece in pieces:
        for first in range(0, piece.shape[0], planes):
            spot = spots[k]
            k += 1
            for p in range(planes):
                hi, lo = split(piece[first + p])
                g_hi[spot, :, p * AREA:(p + 1) * AREA] = hi
                g_lo[spot, :, p * AREA:(p + 1) * AREA] = lo


def spread(sums):
    channels = sums.shape[0] // len(SHIFTS)
    total = jnp.zeros((channels, AREA), F32)
    for b in (-1, 0, 1):
        row = jnp.zeros((channels, AREA), F32)
        for c in (-1, 0, 1):
            s = SHIFTS.index((b, c)) * channels
            row += moved_cells(sums[s:s + channels, :], 0, -c)
        total += moved_cells(row, -b, 0)
    return total


def three_products(w_hi, w_lo, hi, lo):
    out = jnp.dot(w_hi, hi, preferred_element_type=F32)
    out += jnp.dot(w_hi, lo, preferred_element_type=F32)
    return out + jnp.dot(w_lo, hi, preferred_element_type=F32)


def plane_of(g_ref, p):
    lanes = pl.ds(pl.multiple_of(p * AREA, AREA), AREA)
    return g_ref[:, :, lanes].reshape(g_ref.shape[0] * g_ref.shape[1], AREA)


def outer_part(g_hi, g_lo, copies, before_ref, behind_ref, edge_refs=()):
    last = g_hi.shape[2] // AREA - 1
    w_refs = arrived(copies)
    for p, w_hi, w_lo, out in ((0, *w_refs[:2], before_ref), (last, *w_refs[2:], behind_ref)):
        out[0] = spread(three_products(w_hi[...], w_lo[...], plane_of(g_hi, p), plane_of(g_lo, p)))
        for n, edge in enumerate(edge_refs):
            out[n + 1] = edge[p]


def inner_part(copies, g_hi, g_lo, own_ref, sums):
    planes = own_ref.shape[0]
    third = sums.shape[1]
    for n, a in enumerate((1, 0, 2)):
        w_hi, w_lo = arrived(copies[2 * n:2 * n + 2])

        def one_plane(p, _):
            out = three_products(w_hi[...], w_lo[...], plane_of(g_hi, p), plane_of(g_lo, p))
            if a == 1:
                sums[p] = out
            else:
                sums[p + a - 1] += out
            return 0

        lax.fori_loop(max(0, 1 - a), planes - max(0, a - 1), one_plane, 0)

    def one_out(p, _):
        own_ref[p] = spread(sums[p])
        return 0

    lax.fori_loop(0, planes, one_out, 0)


def filter_part(g_hi, g_lo, i_hi, i_lo, outs):
    total = g_hi.shape[0] * g_hi.shape[1]
    planes = g_hi.shape[2] // AREA
    width = total // len(outs)
    for out in outs:
        out[...] = jnp.zeros_like(out)

    def one_plane(p, _):
        lanes = pl.ds(pl.multiple_of(p * AREA, AREA), AREA)
        hi = g_hi[:, :, lanes].reshape(total, AREA)
        lo = g_lo[:, :, lanes].reshape(total, AREA)
        windows = [pl.ds(pl.multiple_of((p + a) * AREA, AREA), AREA) for a in range(3)]
        left_hi = jnp.concatenate([i_hi[:, w] for w in windows], 0)
        left_lo = jnp.concatenate([i_lo[:, w] for w in windows], 0)
        dims = (((1,), (1,)), ((), ()))
        part = lax.dot_general(left_hi, hi, dims, preferred_element_type=F32)
        part += lax.dot_general(left_hi, lo, dims, preferred_element_type=F32)
        part += lax.dot_general(left_lo, hi, dims, preferred_element_type=F32)
        for d, out in enumerate(outs):
            out[...] += part[:, d * width:(d + 1) * width]
        return 0

    lax.fori_loop(0, planes, one_plane, 0)


def first_use(body, spots, pieces, others, outs, flops, name, fetched):
    planes, channels, area = pieces[0].shape
    n, m = len(pieces), len(pieces) + len(others)
    shards = sum(piece.shape[0] for piece in pieces) // planes
    halves = [shape(shards, channels, planes * area, dtype=BF16)] * 2

    def kernel(copies, spots, *refs):
        g_hi, g_lo = refs[m:m + 2]
        gather_blocks(spots, refs[:n], g_hi, g_lo)
        body(g_hi, g_lo, copies, *refs[n:m], *refs[m + 2:])

    g_hi, g_lo, *rest = call(kernel, halves + outs, [], [spots, *pieces, *others], 1, flops, name, fetched)
    return (g_hi, g_lo), rest


def inner(halves, weights, planes, flops, name):
    third = weights[0].shape[0]
    channels = third // len(SHIFTS)
    return call(inner_part, shape(planes, channels, AREA), [pltpu.VMEM((planes, third, AREA), F32)], list(halves),
                0, flops, name, [*weights[2:4], *weights[:2], *weights[4:]])


def turned_kernel(spots, a, b, c, d, *refs):
    outs, turned = refs[:-1], refs[-1]
    turned[...] = (a[...] + b[...] + c[...] + d[...]).T
    height = outs[0].shape[0]
    for k, out in enumerate(outs):
        out[...] = turned[pl.ds(pl.multiple_of(spots[k] * height, height), height), :]


def turned_sum(spots, parts):
    rows, width = parts[0].shape
    return call(turned_kernel, [shape(width // 4, rows)] * 4, [pltpu.VMEM((width, rows), F32)],
                [spots, *parts], 1, name="turned_sum")


def last_kernel(scale, a, b, c, d, out):
    out[...] = ((a[...] + b[...] + c[...] + d[...]) * scale).T


def last_sum(parts, scale):
    height, rows = parts[0].shape
    return call(lambda *refs: last_kernel(scale, *refs), shape(rows, height), [], parts, name="last_sum")


def first_kernel(own, before, after, slope, out):
    planes = out.shape[0]
    for p in range(planes):
        value = own[p]
        if p == 0:
            value = value + before[0]
        if p == planes - 1:
            value = value + after[0]
        out[p] = value * slope[p]


def input_kernel(own, before, after, out):
    planes = own.shape[0]
    for p in range(planes):
        value = own[p]
        if p == 0:
            value = value + before[0]
        if p == planes - 1:
            value = value + after[0]
        out[p] = value


FAR = [(i, (i + 8) % 16) for i in range(16)]
TWIN = [(i, i ^ 1) for i in range(16)]
UP = [(i, i + 1) for i in range(SLABS - 1)]
DOWN = [(i + 1, i) for i in range(SLABS - 1)]


def along_x(d):
    return [(i, (i & 9) | ((i + 2 * d) & 6)) for i in range(16)]


def along_y(d):
    return [(i, (i + 4 * d) % 16) for i in range(16)]


def along_z(d):
    return [(i, (i & 12) | ((i + d) & 3)) for i in range(16)]


def send(value, moves, axis="chan"):
    return lax.ppermute(value, axis, moves)


def after(value, done):
    return lax.optimization_barrier((value, *done))[0]


def shard_ids():
    me = lax.axis_index("chan")
    row, far_row = ([s] + [(s & 9) | ((s - 2 * d) & 6) for d in (1, 3, 2)] for s in (me, me ^ 8))
    ids = row + far_row
    return jnp.stack(ids + [i ^ 1 for i in ids]).astype(jnp.int32)


def gathered(own, soon, late):
    far = send(own, FAR)
    near = [own] + [send(own, along_x(d)) for d in (1, 3, 2)]
    far = after(far, [*near, *soon])
    near_twin = send(jnp.concatenate(near, 0), TWIN)
    wide = [far] + [send(far, along_x(d)) for d in (1, 3, 2)]
    result, done = late(far)
    wide_twin = send(after(jnp.concatenate(wide, 0), done), TWIN)
    return [*near, *wide, near_twin, wide_twin], result


def edges(before, after):
    return send(after, UP, "slab"), send(before, DOWN, "slab")


def row_sum(parts):
    return [parts[0]] + [send(parts[d], along_y(d), "slab") for d in (2, 1, 3)]


def owner_sum(parts, spots, scale):
    rows = turned_sum(spots, parts)
    return last_sum([rows[0]] + [send(rows[d], along_z(d), "slab") for d in (1, 2, 3)], scale)


def per_device(saved_input, pre_first, pre_second, out_grad, weight_first, weight_second):
    saved, pre1, pre2, grad = (jnp.transpose(v, (1, 0, 2)) for v in (saved_input, pre_first, pre_second, out_grad))
    planes, channels, area = saved.shape
    taps, _, total = weight_first.shape
    rows = taps * channels
    flops = 6 * rows * total * planes * area
    scale = 1.0 / math.sqrt(planes * SLABS * area)
    slab = lax.axis_index("slab")
    turn = ((slab // 4 + jnp.arange(4)) % 4).astype(jnp.int32)
    z_spots = ((slab + jnp.arange(4)) % 4).astype(jnp.int32)
    ids = shard_ids()
    spots = (((ids // 4 - slab // 4) % 4) * 4 + ids % 4).astype(jnp.int32)
    quarters = [shape(rows, total // 4)] * 4
    second_grad = scaled(pre2, grad)
    w2, w1, slope = weight_halves(turn, pre1, weight_first, weight_second)
    pieces, _ = gathered(second_grad, [*w1, *w2, slope], lambda far: ((), []))

    halves, (before, behind) = first_use(
        lambda g_hi, g_lo, copies, pre, saved, *outs: outer_part(g_hi, g_lo, copies, *outs, (pre, saved)),
        spots, pieces, [pre1, saved], [shape(3, channels, area)] * 2, flops // 9, "second_outer", [*w2[:2], *w2[4:]])
    before, behind = edges(before, behind)
    own = inner(halves, w2, planes, flops, "second_inner")
    first_grad = call(first_kernel, shape(planes, channels, area), [], [own, before, behind, slope], name="first_grad")
    h_hi, h_lo, x_hi, x_lo = input_halves(pre1, saved, before, behind)

    second_parts = call(lambda g_hi, g_lo, i_hi, i_lo, *outs: filter_part(g_hi, g_lo, i_hi, i_lo, outs),
                        quarters, [], [*halves, h_hi, h_lo], 0, flops, "second_filter")

    def second_sum(far):
        rows = row_sum(lax.optimization_barrier((*second_parts, far))[:4])
        return rows, rows[1:3]

    pieces, second_rows = gathered(first_grad, second_parts, second_sum)
    halves, first_parts = first_use(
        lambda g_hi, g_lo, copies, *outs: filter_part(g_hi, g_lo, *arrived(copies), outs),
        spots, pieces, [], quarters, flops, "first_filter", [x_hi, x_lo])
    first_rows = row_sum(first_parts)
    second_rows = lax.optimization_barrier((*second_rows, first_parts[0]))[:4]
    second_weights = owner_sum(second_rows, z_spots, scale)

    before, behind = call(lambda copies, g_hi, g_lo, *outs: outer_part(g_hi, g_lo, copies, *outs),
                          [shape(1, channels, area)] * 2, [], list(halves), 0, flops // 9, "first_outer",
                          [*w1[:2], *w1[4:]])
    before, behind = edges(before, behind)
    own = inner(halves, w1, planes, flops, "first_inner")
    input_grad = call(input_kernel, shape(planes, channels, area), [], [own, before, behind], name="input_grad")
    first_weights = owner_sum(first_rows, z_spots, scale)
    return (jnp.transpose(input_grad, (1, 0, 2)), first_weights.reshape(taps, channels, -1),
            second_weights.reshape(taps, channels, -1))


def solution(mesh):
    in_specs = (
        P("chan", "slab", None),
        P("chan", "slab", None),
        P("chan", "slab", None),
        P("chan", "slab", None),
        P(None, "chan", None),
        P(None, "chan", None),
    )
    out_specs = (P("chan", "slab", None), P(None, "chan", "slab"), P(None, "chan", "slab"))
    return jax.shard_map(
        per_device, mesh=mesh, in_specs=in_specs, out_specs=out_specs, check_vma=False
    )
```

```python
import math

import jax
import jax.numpy as jnp
from jax import lax
from jax.experimental import pallas as pl
from jax.experimental.pallas import tpu as pltpu
from jax.sharding import PartitionSpec as P

SIDE = 16
AREA = 256
SLABS = 16
SHIFTS = [(b, c) for b in (-1, 0, 1) for c in (-1, 0, 1)]
F32 = jnp.float32
BF16 = jnp.bfloat16
VM = pl.BlockSpec(memory_space=pltpu.VMEM)
SM = pl.BlockSpec(memory_space=pltpu.SMEM)


def slope_of(values):
    sigma = jax.nn.sigmoid(values)
    return sigma * (1.0 + values * (1.0 - sigma))


def call(kernel, out_shape, scratch, args, n_smem=0, flops=0, name=None, fetched=(), vmem=16):
    many = isinstance(out_shape, list)
    moved = sum(a.size * a.dtype.itemsize for a in (*args, *fetched))
    moved += sum(o.size * o.dtype.itemsize for o in (out_shape if many else [out_shape]))
    n, m = len(args), len(fetched)

    def whole(*refs):
        sources, rest = refs[n:n + m], refs[n + m:]
        rest, targets, sems = rest[:len(rest) - m - 1], rest[len(rest) - m - 1:-1], rest[-1]
        copies = [(pltpu.make_async_copy(s, t, sems.at[k]), t) for k, (s, t) in enumerate(zip(sources, targets))]
        for copy, _ in copies:
            copy.start()
        kernel(copies, *refs[:n], *rest)

    if fetched:
        scratch = [*scratch, *(pltpu.VMEM(f.shape, f.dtype) for f in fetched), pltpu.SemaphoreType.DMA((m,))]
    return pl.pallas_call(
        whole if fetched else kernel,
        out_shape=out_shape,
        in_specs=[SM] * n_smem + [VM] * (n - n_smem) + [pl.BlockSpec(memory_space=pltpu.HBM)] * m,
        out_specs=[VM] * len(out_shape) if many else VM,
        scratch_shapes=scratch,
        compiler_params=pltpu.CompilerParams(vmem_limit_bytes=vmem << 20),
        cost_estimate=pl.CostEstimate(flops=flops, bytes_accessed=moved, transcendentals=0),
        name=name,
    )(*args, *fetched)


def arrived(copies):
    for copy, _ in copies:
        copy.wait()
    return [target for _, target in copies]


def shape(*dims, dtype=F32):
    return jax.ShapeDtypeStruct(dims, dtype)


def split(value):
    high = value.astype(BF16)
    return high, (value - high.astype(F32)).astype(BF16)


def moved_cells(plane, row_step, col_step):
    cells = lax.broadcasted_iota(jnp.int32, plane.shape, 1)
    if col_step:
        col = cells % SIDE + col_step
        plane = jnp.where((col >= 0) & (col < SIDE), pltpu.roll(plane, -col_step % AREA, 1), 0.0)
    if row_step:
        row = cells // SIDE + row_step
        plane = jnp.where((row >= 0) & (row < SIDE), pltpu.roll(plane, -row_step * SIDE % AREA, 1), 0.0)
    return plane


def weights_kernel(turn, source, *outs):
    taps, channels, total = source.shape
    width = total // 4
    for a in range(3):
        hi_ref, lo_ref = outs[2 * a:2 * a + 2]

        def one_tap(t, _):
            at = pl.ds(pl.multiple_of(t * channels, channels), channels)
            for d in range(4):
                lanes = pl.ds(pl.multiple_of(turn[d] * width, width), width)
                hi, lo = split(source[t + a * (taps // 3), :, lanes])
                hi_ref[at, d * width:(d + 1) * width] = hi
                lo_ref[at, d * width:(d + 1) * width] = lo
            return 0

        lax.fori_loop(0, taps // 3, one_tap, 0)


def weight_halves(turn, weight, name):
    taps, channels, total = weight.shape
    flat = shape(taps // 3 * channels, total, dtype=BF16)
    return call(weights_kernel, [flat] * 6, [], [turn, weight], 1, name=name)


def second_kernel(turn, source, pre, saved, *outs):
    *halves, rims, slope = outs
    for n, p in enumerate((0, slope.shape[0] - 1)):
        rims[n, 0] = pre[p]
        rims[n, 1] = saved[p]
    slope[...] = slope_of(pre[...])
    weights_kernel(turn, source, *halves)


def second_ready(turn, weight, pre, saved):
    taps, channels, total = weight.shape
    outs = [shape(taps // 3 * channels, total, dtype=BF16)] * 6 + [shape(2, 2, *pre.shape[1:]), shape(*pre.shape)]
    return call(second_kernel, outs, [], [turn, weight, pre, saved], 1, name="second_ready")


def inputs_kernel(n, own_ref, low_ref, high_ref, hi_ref, lo_ref, rows):
    planes, channels, _ = own_ref.shape
    rows[0] = low_ref[n + 1]
    rows[planes + 1] = high_ref[n + 1]
    rows[1:planes + 1] = own_ref[...]

    def one_plane(q, _):
        plane = rows[q]
        if n == 0:
            plane = plane * jax.nn.sigmoid(plane)
        lanes = pl.ds(pl.multiple_of(q * AREA, AREA), AREA)
        for s, (b, c) in enumerate(SHIFTS):
            hi, lo = split(moved_cells(plane, b, c))
            hi_ref[s * channels:(s + 1) * channels, lanes] = hi
            lo_ref[s * channels:(s + 1) * channels, lanes] = lo
        return 0

    lax.fori_loop(0, planes + 2, one_plane, 0)


def input_halves(n, own, low, high, name):
    planes, channels, area = own.shape
    tall = shape(len(SHIFTS) * channels, (planes + 2) * area, dtype=BF16)
    return call(lambda *refs: inputs_kernel(n, *refs), [tall] * 2, [pltpu.VMEM((planes + 2, channels, area), F32)],
                [own, low, high], name=name)


def gather_blocks(spots, pieces, g_hi, g_lo):
    planes = pieces[0].shape[0]
    k = 0
    for piece in pieces:
        for first in range(0, piece.shape[0], planes):
            spot = spots[k]
            k += 1
            for p in range(planes):
                hi, lo = split(piece[first + p])
                g_hi[spot, :, p * AREA:(p + 1) * AREA] = hi
                g_lo[spot, :, p * AREA:(p + 1) * AREA] = lo


def spread(sums):
    channels = sums.shape[0] // len(SHIFTS)
    total = jnp.zeros((channels, AREA), F32)
    for b in (-1, 0, 1):
        row = jnp.zeros((channels, AREA), F32)
        for c in (-1, 0, 1):
            s = SHIFTS.index((b, c)) * channels
            row += moved_cells(sums[s:s + channels, :], 0, -c)
        total += moved_cells(row, -b, 0)
    return total


def three_products(w_hi, w_lo, hi, lo):
    out = jnp.dot(w_hi, hi, preferred_element_type=F32)
    out += jnp.dot(w_hi, lo, preferred_element_type=F32)
    return out + jnp.dot(w_lo, hi, preferred_element_type=F32)


def plane_of(g_ref, p):
    lanes = pl.ds(pl.multiple_of(p * AREA, AREA), AREA)
    return g_ref[:, :, lanes].reshape(g_ref.shape[0] * g_ref.shape[1], AREA)


def outer_part(g_hi, g_lo, w_refs, before_ref, behind_ref, rims=None):
    last = g_hi.shape[2] // AREA - 1
    for p, w_hi, w_lo, out in ((0, *w_refs[:2], before_ref), (last, *w_refs[2:], behind_ref)):
        out[0] = spread(three_products(w_hi[...], w_lo[...], plane_of(g_hi, p), plane_of(g_lo, p)))
        if rims is not None:
            out[1:] = rims[min(p, 1)]


def inner_part(g_hi, g_lo, *refs):
    weights, (own_ref, sums) = refs[:6], refs[6:]
    planes = own_ref.shape[0]
    third = sums.shape[1]
    for n, a in enumerate((1, 0, 2)):
        w_hi, w_lo = weights[2 * n:2 * n + 2]

        def one_plane(p, _):
            out = three_products(w_hi[...], w_lo[...], plane_of(g_hi, p), plane_of(g_lo, p))
            if a == 1:
                sums[p] = out
            else:
                sums[p + a - 1] += out
            return 0

        lax.fori_loop(max(0, 1 - a), planes - max(0, a - 1), one_plane, 0)

    def one_out(p, _):
        own_ref[p] = spread(sums[p])
        return 0

    lax.fori_loop(0, planes, one_out, 0)


def filter_part(g_hi, g_lo, i_hi, i_lo, outs, quarters):
    planes = g_hi.shape[2] // AREA
    width = outs[0].shape[1]
    blocks = width // g_hi.shape[1]
    for out in outs:
        out[...] = jnp.zeros_like(out)

    def one_plane(p, _):
        lanes = pl.ds(pl.multiple_of(p * AREA, AREA), AREA)
        hi, lo = (jnp.concatenate(
            [g[d * blocks:(d + 1) * blocks, :, lanes].reshape(width, AREA) for d in quarters], 0) for g in (g_hi, g_lo))
        windows = [pl.ds(pl.multiple_of((p + a) * AREA, AREA), AREA) for a in range(3)]
        left_hi = jnp.concatenate([i_hi[:, w] for w in windows], 0)
        left_lo = jnp.concatenate([i_lo[:, w] for w in windows], 0)
        dims = (((1,), (1,)), ((), ()))
        part = lax.dot_general(left_hi, hi, dims, preferred_element_type=F32)
        part += lax.dot_general(left_hi, lo, dims, preferred_element_type=F32)
        part += lax.dot_general(left_lo, hi, dims, preferred_element_type=F32)
        for n, out in enumerate(outs):
            out[...] += part[:, n * width:(n + 1) * width]
        return 0

    lax.fori_loop(0, planes, one_plane, 0)


def first_use(body, spots, pieces, others, outs, flops, name, fetched, vmem=16):
    planes, channels, area = pieces[0].shape
    n, m = len(pieces), len(pieces) + len(others)
    shards = sum(piece.shape[0] for piece in pieces) // planes
    halves = [shape(shards, channels, planes * area, dtype=BF16)] * 2

    def kernel(*refs):
        copies = refs[0] if fetched else []
        spots, *refs = refs[1:] if fetched else refs
        g_hi, g_lo = refs[m:m + 2]
        gather_blocks(spots, refs[:n], g_hi, g_lo)
        body(g_hi, g_lo, copies, *refs[n:m], *refs[m + 2:])

    g_hi, g_lo, *rest = call(kernel, halves + outs, [], [spots, *pieces, *others], 1, flops, name, fetched, vmem)
    return (g_hi, g_lo), rest


def inner(halves, weights, planes, flops, name):
    third = weights[0].shape[0]
    channels = third // len(SHIFTS)
    return call(inner_part, shape(planes, channels, AREA), [pltpu.VMEM((planes, third, AREA), F32)],
                [*halves, *weights[2:4], *weights[:2], *weights[4:]], 0, flops, name)


def turned_kernel(spots, a, b, c, d, *refs):
    outs, turned = refs[:-1], refs[-1]
    turned[...] = (a[...] + b[...] + c[...] + d[...]).T
    height = outs[0].shape[0]
    for k, out in enumerate(outs):
        out[...] = turned[pl.ds(pl.multiple_of(spots[k] * height, height), height), :]


def turned_sum(spots, parts):
    rows, width = parts[0].shape
    return call(turned_kernel, [shape(width // 4, rows)] * 4, [pltpu.VMEM((width, rows), F32)],
                [spots, *parts], 1, name="turned_sum")


def last_kernel(scale, a, b, c, d, out):
    out[...] = ((a[...] + b[...] + c[...] + d[...]) * scale).T


def last_sum(parts, scale):
    height, rows = parts[0].shape
    return call(lambda *refs: last_kernel(scale, *refs), shape(rows, height), [], parts, name="last_sum")


def first_kernel(own, before, after, slope, out):
    planes = out.shape[0]
    for p in range(planes):
        value = own[p]
        if p == 0:
            value = value + before[0]
        if p == planes - 1:
            value = value + after[0]
        out[p] = value * slope[p]


def input_kernel(own, before, after, out):
    planes = own.shape[0]
    for p in range(planes):
        value = own[p]
        if p == 0:
            value = value + before[0]
        if p == planes - 1:
            value = value + after[0]
        out[p] = value


FAR = [(i, (i + 8) % 16) for i in range(16)]
TWIN = [(i, i ^ 1) for i in range(16)]
UP = [(i, i + 1) for i in range(SLABS - 1)]
DOWN = [(i + 1, i) for i in range(SLABS - 1)]


def along_x(d):
    return [(i, (i & 9) | ((i + 2 * d) & 6)) for i in range(16)]


def along_y(d):
    return [(i, (i + 4 * d) % 16) for i in range(16)]


def along_z(d):
    return [(i, (i & 12) | ((i + d) & 3)) for i in range(16)]


def send(value, moves, axis="chan"):
    return lax.ppermute(value, axis, moves)


def after(value, done):
    return lax.optimization_barrier((value, *done))[0]


def shard_ids():
    me = lax.axis_index("chan")
    row, far_row = ([s] + [(s & 9) | ((s - 2 * d) & 6) for d in (1, 3, 2)] for s in (me, me ^ 8))
    ids = row + far_row
    return jnp.stack(ids + [i ^ 1 for i in ids]).astype(jnp.int32)


def gathered(own, soon, late):
    far = send(own, FAR)
    near = [own] + [send(own, along_x(d)) for d in (1, 3, 2)]
    far = after(far, [*near[1:3], *soon])
    wide = [far] + [send(far, along_x(d)) for d in (1, 3, 2)]
    near_all = jnp.concatenate(near, 0)
    near_twin = send(near_all, TWIN)
    wide_all = jnp.concatenate(wide, 0)
    result, done = late(far, near_all, wide_all)
    wide_twin = send(after(wide_all, done), TWIN)
    return [*near, *wide, near_twin, wide_twin], result


def edges(before, after):
    return send(after, UP, "slab"), send(before, DOWN, "slab")


def to_row(part, d):
    return send(part, along_y(d), "slab")


def owner_sum(rows, scale):
    return last_sum([rows[0]] + [send(rows[d], along_z(d), "slab") for d in (1, 2, 3)], scale)


def per_device(saved_input, pre_first, pre_second, out_grad, weight_first, weight_second):
    saved, pre1, pre2, grad = (jnp.transpose(v, (1, 0, 2)) for v in (saved_input, pre_first, pre_second, out_grad))
    planes, channels, area = saved.shape
    taps, _, total = weight_first.shape
    rows = taps * channels
    flops = 6 * rows * total * planes * area
    scale = 1.0 / math.sqrt(planes * SLABS * area)
    slab = lax.axis_index("slab")
    turn = ((slab // 4 + jnp.arange(4)) % 4).astype(jnp.int32)
    z_spots = ((slab + jnp.arange(4)) % 4).astype(jnp.int32)
    ids = shard_ids()
    spots = (((ids // 4 - slab // 4) % 4) * 4 + ids % 4).astype(jnp.int32)
    quarter = shape(rows, total // 4)
    second_grad = grad * slope_of(pre2)
    def second_weights_of(_, near, wide):
        return second_ready(after(turn, [wide]), weight_second, pre1, saved), ()

    pieces, (*w2, rims, slope) = gathered(second_grad, [], second_weights_of)

    halves, (before, behind) = first_use(
        lambda g_hi, g_lo, _, rims, *refs: outer_part(g_hi, g_lo, refs[:4], *refs[4:], rims),
        spots, pieces, [rims, *w2[:2], *w2[4:]], [shape(3, channels, area)] * 2, flops // 9, "second_outer", [])
    before, behind = edges(before, behind)
    own = inner(halves, w2, planes, flops, "second_inner")
    first_grad = call(first_kernel, shape(planes, channels, area), [], [own, before, behind, slope], name="first_grad")
    h_hi, h_lo = input_halves(0, pre1, before, behind, "second_input")

    second_parts = call(
        lambda g_hi, g_lo, i_hi, i_lo, *outs: filter_part(g_hi, g_lo, i_hi, i_lo, outs, range(4)),
        [quarter] * 4, [], [*halves, h_hi, h_lo], 0, flops, "second_filter")

    def second_sum(far, near, _):
        parts = lax.optimization_barrier((*second_parts, near))[:4]
        one, three = to_row(parts[1], 1), to_row(parts[3], 3)
        two = to_row(after(parts[2], [one, three]), 2)
        halves = input_halves(1, after(saved, [far]), before, behind, "first_input")
        return ([parts[0], one, two, three], halves), [one, three, *halves]

    pieces, (second_rows, (x_hi, x_lo)) = gathered(first_grad, second_parts, second_sum)
    halves, (part_2, part_1) = first_use(
        lambda g_hi, g_lo, copies, *outs: filter_part(g_hi, g_lo, *arrived(copies), outs, (2, 1)),
        spots, pieces, [], [quarter] * 2, flops // 2, "first_filter", [x_hi, x_lo])
    row_2, row_1 = to_row(part_2, 2), to_row(part_1, 1)
    part_3, part_0 = call(
        lambda g_hi, g_lo, i_hi, i_lo, *outs: filter_part(g_hi, g_lo, i_hi, i_lo, outs, (3, 0)),
        [quarter] * 2, [], [*halves, x_hi, x_lo], 0, flops // 2, "first_filter_rest")
    first_rows = [part_0, row_1, row_2, to_row(part_3, 3)]

    second_rows = lax.optimization_barrier((*second_rows, part_0))[:4]
    second_rows = turned_sum(z_spots, second_rows)
    w1 = weight_halves(after(turn, [second_rows[0]]), weight_first, "first_weights")
    own = inner(halves, w1, planes, flops, "first_inner")
    first_rows = lax.optimization_barrier((*first_rows, own))[:4]
    first_rows = turned_sum(z_spots, first_rows)
    before, behind = call(
        lambda g_hi, g_lo, *refs: outer_part(g_hi, g_lo, refs[:4], *refs[4:]), [shape(1, channels, area)] * 2, [],
        [after(halves[0], [first_rows[0]]), halves[1], *w1[:2], *w1[4:]], 0, flops // 9, "first_outer")
    second_weights = owner_sum(second_rows, scale)
    first_weights = owner_sum(first_rows, scale)
    before, behind = edges(before, behind)
    input_grad = call(input_kernel, shape(planes, channels, area), [], [own, before, behind], name="input_grad")
    return (jnp.transpose(input_grad, (1, 0, 2)), first_weights.reshape(taps, channels, -1),
            second_weights.reshape(taps, channels, -1))


def solution(mesh):
    in_specs = (
        P("chan", "slab", None),
        P("chan", "slab", None),
        P("chan", "slab", None),
        P("chan", "slab", None),
        P(None, "chan", None),
        P(None, "chan", None),
    )
    out_specs = (P("chan", "slab", None), P(None, "chan", "slab"), P(None, "chan", "slab"))
    return jax.shard_map(
        per_device, mesh=mesh, in_specs=in_specs, out_specs=out_specs, check_vma=False
    )
```

```python
import math

import jax
import jax.numpy as jnp
from jax import lax
from jax.experimental import pallas as pl
from jax.experimental.pallas import tpu as pltpu
from jax.sharding import PartitionSpec as P

SIDE = 16
AREA = 256
SLABS = 16
SHIFTS = [(b, c) for b in (-1, 0, 1) for c in (-1, 0, 1)]
F32 = jnp.float32
BF16 = jnp.bfloat16
VM = pl.BlockSpec(memory_space=pltpu.VMEM)
SM = pl.BlockSpec(memory_space=pltpu.SMEM)


def slope_of(values):
    sigma = jax.nn.sigmoid(values)
    return sigma * (1.0 + values * (1.0 - sigma))


def call(kernel, out_shape, scratch, args, n_smem=0, flops=0, name=None, fetched=(), vmem=16):
    many = isinstance(out_shape, list)
    moved = sum(a.size * a.dtype.itemsize for a in (*args, *fetched))
    moved += sum(o.size * o.dtype.itemsize for o in (out_shape if many else [out_shape]))
    n, m = len(args), len(fetched)

    def whole(*refs):
        sources, rest = refs[n:n + m], refs[n + m:]
        rest, targets, sems = rest[:len(rest) - m - 1], rest[len(rest) - m - 1:-1], rest[-1]
        copies = [(pltpu.make_async_copy(s, t, sems.at[k]), t) for k, (s, t) in enumerate(zip(sources, targets))]
        for copy, _ in copies:
            copy.start()
        kernel(copies, *refs[:n], *rest)

    if fetched:
        scratch = [*scratch, *(pltpu.VMEM(f.shape, f.dtype) for f in fetched), pltpu.SemaphoreType.DMA((m,))]
    return pl.pallas_call(
        whole if fetched else kernel,
        out_shape=out_shape,
        in_specs=[SM] * n_smem + [VM] * (n - n_smem) + [pl.BlockSpec(memory_space=pltpu.HBM)] * m,
        out_specs=[VM] * len(out_shape) if many else VM,
        scratch_shapes=scratch,
        compiler_params=pltpu.CompilerParams(vmem_limit_bytes=vmem << 20),
        cost_estimate=pl.CostEstimate(flops=flops, bytes_accessed=moved, transcendentals=0),
        name=name,
    )(*args, *fetched)


def arrived(copies):
    for copy, _ in copies:
        copy.wait()
    return [target for _, target in copies]


def shape(*dims, dtype=F32):
    return jax.ShapeDtypeStruct(dims, dtype)


def split(value):
    high = value.astype(BF16)
    return high, (value - high.astype(F32)).astype(BF16)


def moved_cells(plane, row_step, col_step):
    cells = lax.broadcasted_iota(jnp.int32, plane.shape, 1)
    if col_step:
        col = cells % SIDE + col_step
        plane = jnp.where((col >= 0) & (col < SIDE), pltpu.roll(plane, -col_step % AREA, 1), 0.0)
    if row_step:
        row = cells // SIDE + row_step
        plane = jnp.where((row >= 0) & (row < SIDE), pltpu.roll(plane, -row_step * SIDE % AREA, 1), 0.0)
    return plane


def weights_kernel(turn, source, *outs):
    taps, channels, total = source.shape
    width = total // 4
    for a in range(3):
        hi_ref, lo_ref = outs[2 * a:2 * a + 2]

        def one_tap(t, _):
            at = pl.ds(pl.multiple_of(t * channels, channels), channels)
            for d in range(4):
                lanes = pl.ds(pl.multiple_of(turn[d] * width, width), width)
                hi, lo = split(source[t + a * (taps // 3), :, lanes])
                hi_ref[at, d * width:(d + 1) * width] = hi
                lo_ref[at, d * width:(d + 1) * width] = lo
            return 0

        lax.fori_loop(0, taps // 3, one_tap, 0)


def weight_halves(turn, weight, name):
    taps, channels, total = weight.shape
    flat = shape(taps // 3 * channels, total, dtype=BF16)
    return call(weights_kernel, [flat] * 6, [], [turn, weight], 1, name=name)


def second_kernel(turn, source, pre, saved, *outs):
    *halves, rims, slope = outs
    for n, p in enumerate((0, slope.shape[0] - 1)):
        rims[n, 0] = pre[p]
        rims[n, 1] = saved[n]
    slope[...] = slope_of(pre[...])
    weights_kernel(turn, source, *halves)


def second_ready(turn, weight, pre, saved):
    taps, channels, total = weight.shape
    outs = [shape(taps // 3 * channels, total, dtype=BF16)] * 6 + [shape(2, 2, *pre.shape[1:]), shape(*pre.shape)]
    return call(second_kernel, outs, [], [turn, weight, pre, saved], 1, name="second_ready")


def inputs_kernel(n, own_ref, low_ref, high_ref, hi_ref, lo_ref, rows):
    planes, channels, _ = own_ref.shape
    rows[0] = low_ref[n + 1]
    rows[planes + 1] = high_ref[n + 1]
    rows[1:planes + 1] = own_ref[...]

    def one_plane(q, _):
        plane = rows[q]
        if n == 0:
            plane = plane * jax.nn.sigmoid(plane)
        lanes = pl.ds(pl.multiple_of(q * AREA, AREA), AREA)
        for s, (b, c) in enumerate(SHIFTS):
            hi, lo = split(moved_cells(plane, b, c))
            hi_ref[s * channels:(s + 1) * channels, lanes] = hi
            lo_ref[s * channels:(s + 1) * channels, lanes] = lo
        return 0

    lax.fori_loop(0, planes + 2, one_plane, 0)


def input_halves(n, own, low, high, name):
    planes, channels, area = own.shape
    tall = shape(len(SHIFTS) * channels, (planes + 2) * area, dtype=BF16)
    return call(lambda *refs: inputs_kernel(n, *refs), [tall] * 2, [pltpu.VMEM((planes + 2, channels, area), F32)],
                [own, low, high], name=name)


def gather_blocks(spots, pieces, g_hi, g_lo):
    planes = pieces[0].shape[0]
    k = 0
    for piece in pieces:
        for first in range(0, piece.shape[0], planes):
            spot = spots[k]
            k += 1
            for p in range(planes):
                hi, lo = split(piece[first + p])
                g_hi[spot, :, p * AREA:(p + 1) * AREA] = hi
                g_lo[spot, :, p * AREA:(p + 1) * AREA] = lo


def spread(sums):
    channels = sums.shape[0] // len(SHIFTS)
    total = jnp.zeros((channels, AREA), F32)
    for b in (-1, 0, 1):
        row = jnp.zeros((channels, AREA), F32)
        for c in (-1, 0, 1):
            s = SHIFTS.index((b, c)) * channels
            row += moved_cells(sums[s:s + channels, :], 0, -c)
        total += moved_cells(row, -b, 0)
    return total


def three_products(w_hi, w_lo, hi, lo):
    out = jnp.dot(w_hi, hi, preferred_element_type=F32)
    out += jnp.dot(w_hi, lo, preferred_element_type=F32)
    return out + jnp.dot(w_lo, hi, preferred_element_type=F32)


def plane_of(g_ref, p):
    lanes = pl.ds(p * AREA if isinstance(p, int) else pl.multiple_of(p * AREA, AREA), AREA)
    return g_ref[:, :, lanes].reshape(g_ref.shape[0] * g_ref.shape[1], AREA)


def outer_part(g_hi, g_lo, w_refs, before_ref, behind_ref, rims=None):
    last = g_hi.shape[2] // AREA - 1
    for p, w_hi, w_lo, out in ((0, *w_refs[:2], before_ref), (last, *w_refs[2:], behind_ref)):
        out[0] = spread(three_products(w_hi[...], w_lo[...], plane_of(g_hi, p), plane_of(g_lo, p)))
        if rims is not None:
            out[1:] = rims[min(p, 1)]


def inner_part(g_hi, g_lo, *refs):
    weights, (own_ref, sums) = refs[:6], refs[6:]
    planes = own_ref.shape[0]

    def add_up(q, taps):
        total = None
        for a in taps:
            out = three_products(weights[2 * a][...], weights[2 * a + 1][...],
                                 plane_of(g_hi, q + 1 - a), plane_of(g_lo, q + 1 - a))
            total = out if total is None else total + out
        sums[q % 2] = total

    def one_plane(q, _):
        add_up(q, (0, 1, 2))
        own_ref[q - 1] = spread(sums.at[(q - 1) % 2])
        return 0

    add_up(0, (0, 1))
    lax.fori_loop(1, planes - 1, one_plane, 0)
    add_up(planes - 1, (1, 2))
    own_ref[planes - 2] = spread(sums.at[(planes - 2) % 2])
    own_ref[planes - 1] = spread(sums.at[(planes - 1) % 2])


def filter_part(g_hi, g_lo, i_hi, i_lo, outs, quarters):
    planes = g_hi.shape[2] // AREA
    width = outs[0].shape[1]
    blocks = width // g_hi.shape[1]
    for out in outs:
        out[...] = jnp.zeros_like(out)

    def one_plane(p, _):
        lanes = pl.ds(pl.multiple_of(p * AREA, AREA), AREA)
        hi, lo = (jnp.concatenate(
            [g[d * blocks:(d + 1) * blocks, :, lanes].reshape(width, AREA) for d in quarters], 0) for g in (g_hi, g_lo))
        windows = [pl.ds(pl.multiple_of((p + a) * AREA, AREA), AREA) for a in range(3)]
        left_hi = jnp.concatenate([i_hi[:, w] for w in windows], 0)
        left_lo = jnp.concatenate([i_lo[:, w] for w in windows], 0)
        dims = (((1,), (1,)), ((), ()))
        part = lax.dot_general(left_hi, hi, dims, preferred_element_type=F32)
        part += lax.dot_general(left_hi, lo, dims, preferred_element_type=F32)
        part += lax.dot_general(left_lo, hi, dims, preferred_element_type=F32)
        for n, out in enumerate(outs):
            out[...] += part[:, n * width:(n + 1) * width]
        return 0

    lax.fori_loop(0, planes, one_plane, 0)


def first_use(body, spots, pieces, others, outs, flops, name, fetched, vmem=16):
    planes, channels, area = pieces[0].shape
    n, m = len(pieces), len(pieces) + len(others)
    shards = sum(piece.shape[0] for piece in pieces) // planes
    halves = [shape(shards, channels, planes * area, dtype=BF16)] * 2

    def kernel(*refs):
        copies = refs[0] if fetched else []
        spots, *refs = refs[1:] if fetched else refs
        g_hi, g_lo = refs[m:m + 2]
        gather_blocks(spots, refs[:n], g_hi, g_lo)
        body(g_hi, g_lo, copies, *refs[n:m], *refs[m + 2:])

    g_hi, g_lo, *rest = call(kernel, halves + outs, [], [spots, *pieces, *others], 1, flops, name, fetched, vmem)
    return (g_hi, g_lo), rest


def inner(halves, weights, planes, flops, name):
    third = weights[0].shape[0]
    channels = third // len(SHIFTS)
    return call(inner_part, shape(planes, channels, AREA), [pltpu.VMEM((2, third, AREA), F32)],
                [*halves, *weights], 0, flops, name)


def turned_kernel(spots, a, b, c, d, *refs):
    outs, turned = refs[:-1], refs[-1]
    turned[...] = (a[...] + b[...] + c[...] + d[...]).T
    height = outs[0].shape[0]
    for k, out in enumerate(outs):
        out[...] = turned[pl.ds(pl.multiple_of(spots[k] * height, height), height), :]


def turned_sum(spots, parts):
    rows, width = parts[0].shape
    return call(turned_kernel, [shape(width // 4, rows)] * 4, [pltpu.VMEM((width, rows), F32)],
                [spots, *parts], 1, name="turned_sum")


def last_kernel(scale, a, b, c, d, out):
    out[...] = ((a[...] + b[...] + c[...] + d[...]) * scale).T


def last_sum(parts, scale):
    height, rows = parts[0].shape
    return call(lambda *refs: last_kernel(scale, *refs), shape(rows, height), [], parts, name="last_sum")


def first_kernel(own, before, after, slope, out):
    planes = out.shape[0]
    for p in range(planes):
        value = own[p]
        if p == 0:
            value = value + before[0]
        if p == planes - 1:
            value = value + after[0]
        out[p] = value * slope[p]


def input_kernel(own, before, after, out):
    planes = own.shape[0]
    for p in range(planes):
        value = own[p]
        if p == 0:
            value = value + before[0]
        if p == planes - 1:
            value = value + after[0]
        out[p] = value


FAR = [(i, (i + 8) % 16) for i in range(16)]
TWIN = [(i, i ^ 1) for i in range(16)]
UP = [(i, i + 1) for i in range(SLABS - 1)]
DOWN = [(i + 1, i) for i in range(SLABS - 1)]


def along_x(d):
    return [(i, (i & 9) | ((i + 2 * d) & 6)) for i in range(16)]


def along_y(d):
    return [(i, (i + 4 * d) % 16) for i in range(16)]


def along_z(d):
    return [(i, (i & 12) | ((i + d) & 3)) for i in range(16)]


def send(value, moves, axis="chan"):
    return lax.ppermute(value, axis, moves)


def after(value, done):
    return lax.optimization_barrier((value, *done))[0]


def shard_ids():
    me = lax.axis_index("chan")
    row, far_row = ([s] + [(s & 9) | ((s - 2 * d) & 6) for d in (1, 3, 2)] for s in (me, me ^ 8))
    ids = row + far_row
    return jnp.stack(ids + [i ^ 1 for i in ids]).astype(jnp.int32)


def gathered(own, soon, late):
    far = send(own, FAR)
    near = [own] + [send(own, along_x(d)) for d in (1, 3, 2)]
    far = after(far, [*near[1:3], *soon])
    wide = [far] + [send(far, along_x(d)) for d in (1, 3, 2)]
    near_all = jnp.concatenate(near, 0)
    near_twin = send(near_all, TWIN)
    wide_all = jnp.concatenate(wide, 0)
    result, done = late(far, near_all, wide_all)
    wide_twin = send(after(wide_all, done), TWIN)
    return [*near, *wide, near_twin, wide_twin], result


def edges(before, after):
    return send(after, UP, "slab"), send(before, DOWN, "slab")


def to_row(part, d):
    return send(part, along_y(d), "slab")


def owner_sum(rows, scale):
    return last_sum([rows[0]] + [send(rows[d], along_z(d), "slab") for d in (1, 2, 3)], scale)


def per_device(saved_input, pre_first, pre_second, out_grad, weight_first, weight_second):
    saved, pre1, pre2, grad = (jnp.transpose(v, (1, 0, 2)) for v in (saved_input, pre_first, pre_second, out_grad))
    planes, channels, area = saved.shape
    taps, _, total = weight_first.shape
    rows = taps * channels
    flops = 6 * rows * total * planes * area
    scale = 1.0 / math.sqrt(planes * SLABS * area)
    slab = lax.axis_index("slab")
    turn = ((slab // 4 + jnp.arange(4)) % 4).astype(jnp.int32)
    z_spots = ((slab + jnp.arange(4)) % 4).astype(jnp.int32)
    ids = shard_ids()
    spots = (((ids // 4 - slab // 4) % 4) * 4 + ids % 4).astype(jnp.int32)
    quarter = shape(rows, total // 4)
    second_grad = grad * slope_of(pre2)
    def second_weights_of(_, near, wide):
        return second_ready(after(turn, [wide]), weight_second, pre1, jnp.stack([saved[0], saved[planes - 1]])), ()

    pieces, (*w2, rims, slope) = gathered(second_grad, [], second_weights_of)

    halves, (before, behind) = first_use(
        lambda g_hi, g_lo, _, rims, *refs: outer_part(g_hi, g_lo, refs[:4], *refs[4:], rims),
        spots, pieces, [rims, *w2[:2], *w2[4:]], [shape(3, channels, area)] * 2, flops // 9, "second_outer", [])
    before, behind = edges(before, behind)
    own = inner(halves, w2, planes, flops, "second_inner")
    first_grad = call(first_kernel, shape(planes, channels, area), [], [own, before, behind, slope], name="first_grad")
    h_hi, h_lo = input_halves(0, pre1, before, behind, "second_input")

    second_parts = call(
        lambda g_hi, g_lo, i_hi, i_lo, *outs: filter_part(g_hi, g_lo, i_hi, i_lo, outs, range(4)),
        [quarter] * 4, [], [*halves, h_hi, h_lo], 0, flops, "second_filter")

    def second_sum(far, near, _):
        parts = lax.optimization_barrier((*second_parts, near))[:4]
        one, three = to_row(parts[1], 1), to_row(parts[3], 3)
        two = to_row(after(parts[2], [one, three]), 2)
        halves = input_halves(1, after(saved, [far]), before, behind, "first_input")
        return ([parts[0], one, two, three], halves), [one, three, *halves]

    pieces, (second_rows, (x_hi, x_lo)) = gathered(first_grad, second_parts, second_sum)
    halves, (part_2, part_1) = first_use(
        lambda g_hi, g_lo, copies, *outs: filter_part(g_hi, g_lo, *arrived(copies), outs, (2, 1)),
        spots, pieces, [], [quarter] * 2, flops // 2, "first_filter", [x_hi, x_lo])
    row_2, row_1 = to_row(part_2, 2), to_row(part_1, 1)
    part_3, part_0 = call(
        lambda g_hi, g_lo, i_hi, i_lo, *outs: filter_part(g_hi, g_lo, i_hi, i_lo, outs, (3, 0)),
        [quarter] * 2, [], [*halves, x_hi, x_lo], 0, flops // 2, "first_filter_rest")
    first_rows = [part_0, row_1, row_2, to_row(part_3, 3)]

    second_rows = lax.optimization_barrier((*second_rows, part_0))[:4]
    second_rows = turned_sum(z_spots, second_rows)
    w1 = weight_halves(after(turn, [second_rows[0]]), weight_first, "first_weights")
    before, behind = call(
        lambda g_hi, g_lo, *refs: outer_part(g_hi, g_lo, refs[:4], *refs[4:]), [shape(1, channels, area)] * 2, [],
        [*halves, *w1[:2], *w1[4:]], 0, flops // 9, "first_outer")
    first_rows = lax.optimization_barrier((*first_rows, before))[:4]
    first_rows = turned_sum(z_spots, first_rows)
    own = inner([after(halves[0], [first_rows[0]]), halves[1]], w1, planes, flops, "first_inner")
    second_weights = owner_sum(second_rows, scale)
    first_weights = owner_sum(first_rows, scale)
    before, behind = edges(before, behind)
    input_grad = call(input_kernel, shape(planes, channels, area), [], [own, before, behind], name="input_grad")
    return (jnp.transpose(input_grad, (1, 0, 2)), first_weights.reshape(taps, channels, -1),
            second_weights.reshape(taps, channels, -1))


def solution(mesh):
    in_specs = (
        P("chan", "slab", None),
        P("chan", "slab", None),
        P("chan", "slab", None),
        P("chan", "slab", None),
        P(None, "chan", None),
        P(None, "chan", None),
    )
    out_specs = (P("chan", "slab", None), P(None, "chan", "slab"), P(None, "chan", "slab"))
    return jax.shard_map(
        per_device, mesh=mesh, in_specs=in_specs, out_specs=out_specs, check_vma=False
    )
```

```python
import math

import jax
import jax.numpy as jnp
from jax import lax
from jax.experimental import pallas as pl
from jax.experimental.pallas import tpu as pltpu
from jax.sharding import PartitionSpec as P

SIDE = 16
AREA = 256
SLABS = 16
SHIFTS = [(b, c) for b in (-1, 0, 1) for c in (-1, 0, 1)]
F32 = jnp.float32
BF16 = jnp.bfloat16
VM = pl.BlockSpec(memory_space=pltpu.VMEM)
SM = pl.BlockSpec(memory_space=pltpu.SMEM)


def slope_of(values):
    sigma = jax.nn.sigmoid(values)
    return sigma * (1.0 + values * (1.0 - sigma))


def call(kernel, out_shape, scratch, args, n_smem=0, flops=0, name=None):
    many = isinstance(out_shape, list)
    moved = sum(a.size * a.dtype.itemsize for a in args)
    moved += sum(o.size * o.dtype.itemsize for o in (out_shape if many else [out_shape]))
    return pl.pallas_call(
        kernel,
        out_shape=out_shape,
        in_specs=[SM] * n_smem + [VM] * (len(args) - n_smem),
        out_specs=[VM] * len(out_shape) if many else VM,
        scratch_shapes=scratch,
        compiler_params=pltpu.CompilerParams(vmem_limit_bytes=16 << 20),
        cost_estimate=pl.CostEstimate(flops=flops, bytes_accessed=moved, transcendentals=0),
        name=name,
    )(*args)


def shape(*dims, dtype=F32):
    return jax.ShapeDtypeStruct(dims, dtype)


def split(value):
    high = value.astype(BF16)
    return high, (value - high.astype(F32)).astype(BF16)


def moved_cells(plane, row_step, col_step):
    cells = lax.broadcasted_iota(jnp.int32, plane.shape, 1)
    if col_step:
        col = cells % SIDE + col_step
        plane = jnp.where((col >= 0) & (col < SIDE), pltpu.roll(plane, -col_step % AREA, 1), 0.0)
    if row_step:
        row = cells // SIDE + row_step
        plane = jnp.where((row >= 0) & (row < SIDE), pltpu.roll(plane, -row_step * SIDE % AREA, 1), 0.0)
    return plane


def weights_kernel(turn, source, *outs):
    taps, channels, total = source.shape
    width = total // 4
    for a in range(3):
        hi_ref, lo_ref = outs[2 * a:2 * a + 2]

        def one_tap(t, _):
            at = pl.ds(pl.multiple_of(t * channels, channels), channels)
            for d in range(4):
                lanes = pl.ds(pl.multiple_of(turn[d] * width, width), width)
                hi, lo = split(source[t + a * (taps // 3), :, lanes])
                hi_ref[at, d * width:(d + 1) * width] = hi
                lo_ref[at, d * width:(d + 1) * width] = lo
            return 0

        lax.fori_loop(0, taps // 3, one_tap, 0)


def weight_halves(turn, weight, name):
    taps, channels, total = weight.shape
    flat = shape(taps // 3 * channels, total, dtype=BF16)
    return call(weights_kernel, [flat] * 6, [], [turn, weight], 1, name=name)


def second_kernel(turn, source, pre, saved, *outs):
    *halves, rims, slope = outs
    for n, p in enumerate((0, slope.shape[0] - 1)):
        rims[n, 0] = pre[p]
        rims[n, 1] = saved[n]
    slope[...] = slope_of(pre[...])
    weights_kernel(turn, source, *halves)


def second_ready(turn, weight, pre, saved):
    taps, channels, total = weight.shape
    outs = [shape(taps // 3 * channels, total, dtype=BF16)] * 6 + [shape(2, 2, *pre.shape[1:]), shape(*pre.shape)]
    return call(second_kernel, outs, [], [turn, weight, pre, saved], 1, name="second_ready")


def inputs_kernel(n, own_ref, low_ref, high_ref, hi_ref, lo_ref, rows):
    planes, channels, _ = own_ref.shape
    rows[0] = low_ref[n + 1]
    rows[planes + 1] = high_ref[n + 1]
    rows[1:planes + 1] = own_ref[...]

    def one_plane(q, _):
        plane = rows[q]
        if n == 0:
            plane = plane * jax.nn.sigmoid(plane)
        lanes = pl.ds(pl.multiple_of(q * AREA, AREA), AREA)
        for s, (b, c) in enumerate(SHIFTS):
            hi, lo = split(moved_cells(plane, b, c))
            hi_ref[s * channels:(s + 1) * channels, lanes] = hi
            lo_ref[s * channels:(s + 1) * channels, lanes] = lo
        return 0

    lax.fori_loop(0, planes + 2, one_plane, 0)


def input_halves(n, own, low, high, name):
    planes, channels, area = own.shape
    tall = shape(len(SHIFTS) * channels, (planes + 2) * area, dtype=BF16)
    return call(lambda *refs: inputs_kernel(n, *refs), [tall] * 2, [pltpu.VMEM((planes + 2, channels, area), F32)],
                [own, low, high], name=name)


def lanes_of(p):
    return pl.ds(p * AREA if isinstance(p, int) else pl.multiple_of(p * AREA, AREA), AREA)


def split_plane(spots, pieces, p, planes, g_hi, g_lo):
    k = 0
    for piece in pieces:
        for first in range(0, piece.shape[0], planes):
            hi, lo = split(piece[first + p])
            g_hi[spots[k], :, lanes_of(p)] = hi
            g_lo[spots[k], :, lanes_of(p)] = lo
            k += 1


def spread(sums):
    channels = sums.shape[0] // len(SHIFTS)
    total = jnp.zeros((channels, AREA), F32)
    for b in (-1, 0, 1):
        row = jnp.zeros((channels, AREA), F32)
        for c in (-1, 0, 1):
            s = SHIFTS.index((b, c)) * channels
            row += moved_cells(sums[s:s + channels, :], 0, -c)
        total += moved_cells(row, -b, 0)
    return total


def three_products(w_hi, w_lo, hi, lo):
    out = jnp.dot(w_hi, hi, preferred_element_type=F32)
    out += jnp.dot(w_hi, lo, preferred_element_type=F32)
    return out + jnp.dot(w_lo, hi, preferred_element_type=F32)


def plane_of(g_ref, p):
    return g_ref[:, :, lanes_of(p)].reshape(g_ref.shape[0] * g_ref.shape[1], AREA)


def outer_part(first, last, w_refs, before_ref, behind_ref, rims=None):
    for n, (planes, w_hi, w_lo, out) in enumerate(((first, *w_refs[:2], before_ref), (last, *w_refs[2:], behind_ref))):
        out[0] = spread(three_products(w_hi[...], w_lo[...], *planes))
        if rims is not None:
            out[1:] = rims[n]


def second_outer_kernel(n, spots, *refs):
    pieces, rims, weights, (g_hi, g_lo, before_ref, behind_ref) = refs[:n], refs[n], refs[n + 1:n + 5], refs[n + 5:]
    last = g_hi.shape[2] // AREA - 1
    split_plane(spots, pieces, 0, last + 1, g_hi, g_lo)
    split_plane(spots, pieces, last, last + 1, g_hi, g_lo)
    outer_part(*([plane_of(g, p) for g in (g_hi, g_lo)] for p in (0, last)), weights, before_ref, behind_ref, rims)
    for p in range(1, last):
        split_plane(spots, pieces, p, last + 1, g_hi, g_lo)


def first_outer_kernel(g_hi, g_lo, *refs):
    last = g_hi.shape[2] // AREA - 1
    outer_part(*([plane_of(g, p) for g in (g_hi, g_lo)] for p in (0, last)), refs[:4], *refs[4:])


def inner_part(g_hi, g_lo, *refs):
    weights, (own_ref, sums) = refs[:6], refs[6:]
    planes = own_ref.shape[0]

    def add_up(q, taps):
        total = None
        for a in taps:
            out = three_products(weights[2 * a][...], weights[2 * a + 1][...],
                                 plane_of(g_hi, q + 1 - a), plane_of(g_lo, q + 1 - a))
            total = out if total is None else total + out
        sums[q % 2] = total

    def one_plane(q, _):
        add_up(q, (0, 1, 2))
        own_ref[q - 1] = spread(sums.at[(q - 1) % 2])
        return 0

    add_up(0, (0, 1))
    lax.fori_loop(1, planes - 1, one_plane, 0)
    add_up(planes - 1, (1, 2))
    own_ref[planes - 2] = spread(sums.at[(planes - 2) % 2])
    own_ref[planes - 1] = spread(sums.at[(planes - 1) % 2])


def filter_add(p, hi, lo, i_hi, i_lo, outs):
    width = outs[0].shape[1]
    left_hi, left_lo = (jnp.concatenate([i[:, lanes_of(p + a)] for a in range(3)], 0) for i in (i_hi, i_lo))
    dims = (((1,), (1,)), ((), ()))
    part = lax.dot_general(left_hi, hi, dims, preferred_element_type=F32)
    part += lax.dot_general(left_hi, lo, dims, preferred_element_type=F32)
    part += lax.dot_general(left_lo, hi, dims, preferred_element_type=F32)
    for n, out in enumerate(outs):
        out[...] += part[:, n * width:(n + 1) * width]


def quarters_of(g_ref, p, quarters):
    blocks = g_ref.shape[0] // 4
    width = blocks * g_ref.shape[1]
    return jnp.concatenate([g_ref[d * blocks:(d + 1) * blocks, :, lanes_of(p)].reshape(width, AREA) for d in quarters], 0)


def filter_kernel(quarters, g_hi, g_lo, i_hi, i_lo, *outs):
    for out in outs:
        out[...] = jnp.zeros_like(out)

    for p in range(g_hi.shape[2] // AREA):
        filter_add(p, quarters_of(g_hi, p, quarters), quarters_of(g_lo, p, quarters), i_hi, i_lo, outs)


def filter_quarters(quarters, halves, inputs, flops, name):
    rows, total = 3 * inputs[0].shape[0], halves[0].shape[0] * halves[0].shape[1]
    return call(lambda *refs: filter_kernel(quarters, *refs), [shape(rows, total // 4)] * len(quarters), [],
                [*halves, *inputs], 0, flops, name)


def first_filter_kernel(n, quarters, spots, *refs):
    pieces, inputs, (g_hi, g_lo), outs = refs[:n], refs[n:n + 2], refs[n + 2:n + 4], refs[n + 4:n + 4 + len(quarters)]
    planes = g_hi.shape[2] // AREA
    for out in outs:
        out[...] = jnp.zeros_like(out)
    split_plane(spots, pieces, 0, planes, g_hi, g_lo)
    for p in range(planes):
        filter_add(p, quarters_of(g_hi, p, quarters), quarters_of(g_lo, p, quarters), *inputs, outs)
        if p + 1 < planes:
            split_plane(spots, pieces, p + 1, planes, g_hi, g_lo)


def first_use(kernel, spots, pieces, others, outs, flops, name):
    planes, channels, area = pieces[0].shape
    shards = sum(piece.shape[0] for piece in pieces) // planes
    halves = [shape(shards, channels, planes * area, dtype=BF16)] * 2
    g_hi, g_lo, *rest = call(kernel, halves + outs, [], [spots, *pieces, *others], 1, flops, name)
    return (g_hi, g_lo), rest


def inner(halves, weights, planes, flops, name):
    third = weights[0].shape[0]
    channels = third // len(SHIFTS)
    return call(inner_part, shape(planes, channels, AREA), [pltpu.VMEM((2, third, AREA), F32)],
                [*halves, *weights], 0, flops, name)


def turned_kernel(spots, a, b, c, d, *refs):
    outs, turned = refs[:-1], refs[-1]
    turned[...] = (a[...] + b[...] + c[...] + d[...]).T
    height = outs[0].shape[0]
    for k, out in enumerate(outs):
        out[...] = turned[pl.ds(pl.multiple_of(spots[k] * height, height), height), :]


def turned_sum(spots, parts):
    rows, width = parts[0].shape
    return call(turned_kernel, [shape(width // 4, rows)] * 4, [pltpu.VMEM((width, rows), F32)],
                [spots, *parts], 1, name="turned_sum")


def last_kernel(scale, a, b, c, d, out):
    out[...] = ((a[...] + b[...] + c[...] + d[...]) * scale).T


def last_sum(parts, scale):
    height, rows = parts[0].shape
    return call(lambda *refs: last_kernel(scale, *refs), shape(rows, height), [], parts, name="last_sum")


def first_kernel(own, before, after, slope, out):
    planes = out.shape[0]
    for p in range(planes):
        value = own[p]
        if p == 0:
            value = value + before[0]
        if p == planes - 1:
            value = value + after[0]
        out[p] = value * slope[p]


def input_kernel(own, before, after, out):
    planes = own.shape[0]
    for p in range(planes):
        value = own[p]
        if p == 0:
            value = value + before[0]
        if p == planes - 1:
            value = value + after[0]
        out[p] = value


FAR = [(i, (i + 8) % 16) for i in range(16)]
TWIN = [(i, i ^ 1) for i in range(16)]
UP = [(i, i + 1) for i in range(SLABS - 1)]
DOWN = [(i + 1, i) for i in range(SLABS - 1)]


def along_x(d):
    return [(i, (i & 9) | ((i + 2 * d) & 6)) for i in range(16)]


def along_y(d):
    return [(i, (i + 4 * d) % 16) for i in range(16)]


def along_z(d):
    return [(i, (i & 12) | ((i + d) & 3)) for i in range(16)]


def send(value, moves, axis="chan"):
    return lax.ppermute(value, axis, moves)


def after(value, done):
    return lax.optimization_barrier((value, *done))[0]


def shard_ids():
    me = lax.axis_index("chan")
    row, far_row = ([s] + [(s & 9) | ((s - 2 * d) & 6) for d in (1, 3, 2)] for s in (me, me ^ 8))
    ids = row + far_row
    return jnp.stack(ids + [i ^ 1 for i in ids]).astype(jnp.int32)


def gathered(own, soon, late):
    far = send(own, FAR)
    near = [own] + [send(own, along_x(d)) for d in (1, 3, 2)]
    far = after(far, [*near[1:3], *soon])
    wide = [far] + [send(far, along_x(d)) for d in (1, 3, 2)]
    near_all = jnp.concatenate(near, 0)
    near_twin = send(near_all, TWIN)
    wide_all = jnp.concatenate(wide, 0)
    result, done = late(far, near_all, wide_all)
    wide_twin = send(after(wide_all, done), TWIN)
    return [*near, *wide, near_twin, wide_twin], result


def edges(before, after):
    return send(after, UP, "slab"), send(before, DOWN, "slab")


def to_row(part, d):
    return send(part, along_y(d), "slab")


def to_owners(rows):
    return [rows[0]] + [send(rows[d], along_z(d), "slab") for d in (1, 2, 3)]


def per_device(saved_input, pre_first, pre_second, out_grad, weight_first, weight_second):
    saved, pre1, pre2, grad = (jnp.transpose(v, (1, 0, 2)) for v in (saved_input, pre_first, pre_second, out_grad))
    planes, channels, area = saved.shape
    taps, _, total = weight_first.shape
    rows = taps * channels
    flops = 6 * rows * total * planes * area
    scale = 1.0 / math.sqrt(planes * SLABS * area)
    slab = lax.axis_index("slab")
    turn = ((slab // 4 + jnp.arange(4)) % 4).astype(jnp.int32)
    z_spots = ((slab + jnp.arange(4)) % 4).astype(jnp.int32)
    ids = shard_ids()
    spots = (((ids // 4 - slab // 4) % 4) * 4 + ids % 4).astype(jnp.int32)
    quarter = shape(rows, total // 4)
    second_grad = grad * slope_of(pre2)
    saved_rims = jnp.stack([saved[0], saved[planes - 1]])

    def second_weights_of(_, near, wide):
        return second_ready(after(turn, [wide]), weight_second, pre1, saved_rims), [saved_rims]

    pieces, (*w2, rims, slope) = gathered(second_grad, [], second_weights_of)

    n = len(pieces)
    halves, (before, behind) = first_use(
        lambda *refs: second_outer_kernel(n, *refs), spots, pieces, [rims, *w2[:2], *w2[4:]],
        [shape(3, channels, area)] * 2, flops // 9, "second_outer")
    before, behind = edges(before, behind)
    own = inner(halves, w2, planes, flops, "second_inner")
    first_grad = call(first_kernel, shape(planes, channels, area), [], [own, before, behind, slope], name="first_grad")
    h_hi, h_lo = input_halves(0, pre1, before, behind, "second_input")

    second_parts = filter_quarters(range(4), halves, (h_hi, h_lo), flops, "second_filter")

    def second_sum(far, near, _):
        parts = lax.optimization_barrier((*second_parts, near))[:4]
        one, three = to_row(parts[1], 1), to_row(parts[3], 3)
        two = to_row(after(parts[2], [one, three]), 2)
        halves = input_halves(1, after(saved, [far]), before, behind, "first_input")
        w1 = weight_halves(after(turn, [far]), weight_first, "first_weights")
        return ([parts[0], one, two, three], halves, w1), [one, three, *halves, *w1]

    pieces, (second_rows, inputs, w1) = gathered(first_grad, second_parts, second_sum)
    halves, (part_2, part_1) = first_use(
        lambda *refs: first_filter_kernel(n, (2, 1), *refs), spots, pieces, inputs, [quarter] * 2, flops // 2,
        "first_filter")
    row_2, row_1 = to_row(part_2, 2), to_row(part_1, 1)
    part_3, part_0 = filter_quarters((3, 0), halves, inputs, flops // 2, "first_filter_rest")
    first_rows = [part_0, row_1, row_2, to_row(part_3, 3)]

    second_rows = lax.optimization_barrier((*second_rows, part_0))[:4]
    second_rows = turned_sum(z_spots, second_rows)
    own = inner(halves, w1, planes, flops, "first_inner")
    first_rows = lax.optimization_barrier((*first_rows, own))[:4]
    first_rows = turned_sum(z_spots, first_rows)
    before, behind = call(first_outer_kernel, [shape(1, channels, area)] * 2, [],
                          [after(halves[0], [first_rows[0]]), halves[1], *w1[:2], *w1[4:]], 0, flops // 9, "first_outer")
    second_rows = lax.optimization_barrier((*to_owners(second_rows), first_rows[0]))[:4]
    second_weights = last_sum(second_rows, scale)
    first_weights = last_sum(to_owners(first_rows), scale)
    before, behind = edges(before, behind)
    input_grad = call(input_kernel, shape(planes, channels, area), [], [own, before, behind], name="input_grad")
    return (jnp.transpose(input_grad, (1, 0, 2)), first_weights.reshape(taps, channels, -1),
            second_weights.reshape(taps, channels, -1))


def solution(mesh):
    in_specs = (
        P("chan", "slab", None),
        P("chan", "slab", None),
        P("chan", "slab", None),
        P("chan", "slab", None),
        P(None, "chan", None),
        P(None, "chan", None),
    )
    out_specs = (P("chan", "slab", None), P(None, "chan", "slab"), P(None, "chan", "slab"))
    return jax.shard_map(
        per_device, mesh=mesh, in_specs=in_specs, out_specs=out_specs, check_vma=False
    )
```

```python
import math

import jax
import jax.numpy as jnp
from jax import lax
from jax.experimental import pallas as pl
from jax.experimental.pallas import tpu as pltpu
from jax.sharding import PartitionSpec as P

SIDE = 16
AREA = 256
SLABS = 16
SHIFTS = [(b, c) for b in (-1, 0, 1) for c in (-1, 0, 1)]
F32 = jnp.float32
BF16 = jnp.bfloat16
VM = pl.BlockSpec(memory_space=pltpu.VMEM)
SM = pl.BlockSpec(memory_space=pltpu.SMEM)


def slope_of(values):
    sigma = jax.nn.sigmoid(values)
    return sigma * (1.0 + values * (1.0 - sigma))


def call(kernel, out_shape, scratch, args, n_smem=0, flops=0, name=None):
    many = isinstance(out_shape, list)
    moved = sum(a.size * a.dtype.itemsize for a in args)
    moved += sum(o.size * o.dtype.itemsize for o in (out_shape if many else [out_shape]))
    return pl.pallas_call(
        kernel,
        out_shape=out_shape,
        in_specs=[SM] * n_smem + [VM] * (len(args) - n_smem),
        out_specs=[VM] * len(out_shape) if many else VM,
        scratch_shapes=scratch,
        compiler_params=pltpu.CompilerParams(vmem_limit_bytes=16 << 20),
        cost_estimate=pl.CostEstimate(flops=flops, bytes_accessed=moved, transcendentals=0),
        name=name,
    )(*args)


def shape(*dims, dtype=F32):
    return jax.ShapeDtypeStruct(dims, dtype)


def split(value):
    high = value.astype(BF16)
    return high, (value - high.astype(F32)).astype(BF16)


def moved_cells(plane, row_step, col_step):
    cells = lax.broadcasted_iota(jnp.int32, plane.shape, 1)
    if col_step:
        col = cells % SIDE + col_step
        plane = jnp.where((col >= 0) & (col < SIDE), pltpu.roll(plane, -col_step % AREA, 1), 0.0)
    if row_step:
        row = cells // SIDE + row_step
        plane = jnp.where((row >= 0) & (row < SIDE), pltpu.roll(plane, -row_step * SIDE % AREA, 1), 0.0)
    return plane


def weights_kernel(turn, source, *outs):
    taps, channels, total = source.shape
    width = total // 4
    for a in range(3):
        hi_ref, lo_ref = outs[2 * a:2 * a + 2]

        def one_tap(t, _):
            at = pl.ds(pl.multiple_of(t * channels, channels), channels)
            for d in range(4):
                lanes = pl.ds(pl.multiple_of(turn[d] * width, width), width)
                hi, lo = split(source[t + a * (taps // 3), :, lanes])
                hi_ref[at, d * width:(d + 1) * width] = hi
                lo_ref[at, d * width:(d + 1) * width] = lo
            return 0

        lax.fori_loop(0, taps // 3, one_tap, 0)


def weight_halves(turn, weight, name):
    taps, channels, total = weight.shape
    flat = shape(taps // 3 * channels, total, dtype=BF16)
    return call(weights_kernel, [flat] * 6, [], [turn, weight], 1, name=name)


def second_kernel(turn, source, pre, saved, *outs):
    *halves, rims, slope = outs
    for n, p in enumerate((0, slope.shape[0] - 1)):
        rims[n, 0] = pre[p]
        rims[n, 1] = saved[n]
    slope[...] = slope_of(pre[...])
    weights_kernel(turn, source, *halves)


def second_ready(turn, weight, pre, saved):
    taps, channels, total = weight.shape
    outs = [shape(taps // 3 * channels, total, dtype=BF16)] * 6 + [shape(2, 2, *pre.shape[1:]), shape(*pre.shape)]
    return call(second_kernel, outs, [], [turn, weight, pre, saved], 1, name="second_ready")


def inputs_kernel(n, own_ref, low_ref, high_ref, hi_ref, lo_ref, rows):
    planes, channels, _ = own_ref.shape
    rows[0] = low_ref[n + 1]
    rows[planes + 1] = high_ref[n + 1]
    rows[1:planes + 1] = own_ref[...]

    def one_plane(q, _):
        plane = rows[q]
        if n == 0:
            plane = plane * jax.nn.sigmoid(plane)
        lanes = pl.ds(pl.multiple_of(q * AREA, AREA), AREA)
        for s, (b, c) in enumerate(SHIFTS):
            hi, lo = split(moved_cells(plane, b, c))
            hi_ref[s * channels:(s + 1) * channels, lanes] = hi
            lo_ref[s * channels:(s + 1) * channels, lanes] = lo
        return 0

    lax.fori_loop(0, planes + 2, one_plane, 0)


def input_halves(n, own, low, high, name):
    planes, channels, area = own.shape
    tall = shape(len(SHIFTS) * channels, (planes + 2) * area, dtype=BF16)
    return call(lambda *refs: inputs_kernel(n, *refs), [tall] * 2, [pltpu.VMEM((planes + 2, channels, area), F32)],
                [own, low, high], name=name)


def lanes_of(p):
    return pl.ds(p * AREA if isinstance(p, int) else pl.multiple_of(p * AREA, AREA), AREA)


def split_plane(spots, pieces, p, planes, g_hi, g_lo):
    k = 0
    for piece in pieces:
        for first in range(0, piece.shape[0], planes):
            hi, lo = split(piece[first + p])
            g_hi[spots[k], :, lanes_of(p)] = hi
            g_lo[spots[k], :, lanes_of(p)] = lo
            k += 1


def spread(sums):
    channels = sums.shape[0] // len(SHIFTS)
    total = jnp.zeros((channels, AREA), F32)
    for b in (-1, 0, 1):
        row = jnp.zeros((channels, AREA), F32)
        for c in (-1, 0, 1):
            s = SHIFTS.index((b, c)) * channels
            row += moved_cells(sums[s:s + channels, :], 0, -c)
        total += moved_cells(row, -b, 0)
    return total


def three_products(w_hi, w_lo, hi, lo):
    out = jnp.dot(w_hi, hi, preferred_element_type=F32)
    out += jnp.dot(w_hi, lo, preferred_element_type=F32)
    return out + jnp.dot(w_lo, hi, preferred_element_type=F32)


def plane_of(g_ref, p):
    return g_ref[:, :, lanes_of(p)].reshape(g_ref.shape[0] * g_ref.shape[1], AREA)


def outer_part(first, last, w_refs, before_ref, behind_ref, rims=None):
    for n, (planes, w_hi, w_lo, out) in enumerate(((first, *w_refs[:2], before_ref), (last, *w_refs[2:], behind_ref))):
        out[0] = spread(three_products(w_hi[...], w_lo[...], *planes))
        if rims is not None:
            out[1:] = rims[n]


def second_outer_kernel(n, spots, *refs):
    pieces, rims, weights, (g_hi, g_lo, before_ref, behind_ref) = refs[:n], refs[n], refs[n + 1:n + 5], refs[n + 5:]
    last = g_hi.shape[2] // AREA - 1
    split_plane(spots, pieces, 0, last + 1, g_hi, g_lo)
    split_plane(spots, pieces, last, last + 1, g_hi, g_lo)
    outer_part(*([plane_of(g, p) for g in (g_hi, g_lo)] for p in (0, last)), weights, before_ref, behind_ref, rims)
    for p in range(1, last):
        split_plane(spots, pieces, p, last + 1, g_hi, g_lo)


def first_outer_kernel(g_hi, g_lo, *refs):
    last = g_hi.shape[2] // AREA - 1
    outer_part(*([plane_of(g, p) for g in (g_hi, g_lo)] for p in (0, last)), refs[:4], *refs[4:])


def inner_part(g_hi, g_lo, *refs):
    weights, (own_ref, sums) = refs[:6], refs[6:]
    planes = own_ref.shape[0]

    def add_up(q, taps):
        total = None
        for a in taps:
            out = three_products(weights[2 * a][...], weights[2 * a + 1][...],
                                 plane_of(g_hi, q + 1 - a), plane_of(g_lo, q + 1 - a))
            total = out if total is None else total + out
        sums[q % 2] = total

    def one_plane(q, _):
        add_up(q, (0, 1, 2))
        own_ref[q - 1] = spread(sums.at[(q - 1) % 2])
        return 0

    add_up(0, (0, 1))
    lax.fori_loop(1, planes - 1, one_plane, 0)
    add_up(planes - 1, (1, 2))
    own_ref[planes - 2] = spread(sums.at[(planes - 2) % 2])
    own_ref[planes - 1] = spread(sums.at[(planes - 1) % 2])


def filter_add(p, hi, lo, i_hi, i_lo, outs):
    width = outs[0].shape[1]
    left_hi, left_lo = (jnp.concatenate([i[:, lanes_of(p + a)] for a in range(3)], 0) for i in (i_hi, i_lo))
    dims = (((1,), (1,)), ((), ()))
    part = lax.dot_general(left_hi, hi, dims, preferred_element_type=F32)
    part += lax.dot_general(left_hi, lo, dims, preferred_element_type=F32)
    part += lax.dot_general(left_lo, hi, dims, preferred_element_type=F32)
    for n, out in enumerate(outs):
        out[...] += part[:, n * width:(n + 1) * width]


def quarters_of(g_ref, p, quarters):
    blocks = g_ref.shape[0] // 4
    width = blocks * g_ref.shape[1]
    return jnp.concatenate([g_ref[d * blocks:(d + 1) * blocks, :, lanes_of(p)].reshape(width, AREA) for d in quarters], 0)


def filter_kernel(quarters, g_hi, g_lo, i_hi, i_lo, *outs):
    for out in outs:
        out[...] = jnp.zeros_like(out)

    for p in range(g_hi.shape[2] // AREA):
        filter_add(p, quarters_of(g_hi, p, quarters), quarters_of(g_lo, p, quarters), i_hi, i_lo, outs)


def filter_quarters(quarters, halves, inputs, flops, name):
    rows, total = 3 * inputs[0].shape[0], halves[0].shape[0] * halves[0].shape[1]
    return call(lambda *refs: filter_kernel(quarters, *refs), [shape(rows, total // 4)] * len(quarters), [],
                [*halves, *inputs], 0, flops, name)


def first_filter_kernel(n, quarters, spots, *refs):
    pieces, inputs, (g_hi, g_lo), outs = refs[:n], refs[n:n + 2], refs[n + 2:n + 4], refs[n + 4:n + 4 + len(quarters)]
    planes = g_hi.shape[2] // AREA
    for out in outs:
        out[...] = jnp.zeros_like(out)
    split_plane(spots, pieces, 0, planes, g_hi, g_lo)
    for p in range(planes):
        filter_add(p, quarters_of(g_hi, p, quarters), quarters_of(g_lo, p, quarters), *inputs, outs)
        if p + 1 < planes:
            split_plane(spots, pieces, p + 1, planes, g_hi, g_lo)


def first_use(kernel, spots, pieces, others, outs, flops, name):
    planes, channels, area = pieces[0].shape
    shards = sum(piece.shape[0] for piece in pieces) // planes
    halves = [shape(shards, channels, planes * area, dtype=BF16)] * 2
    g_hi, g_lo, *rest = call(kernel, halves + outs, [], [spots, *pieces, *others], 1, flops, name)
    return (g_hi, g_lo), rest


def flat_part(g_hi, g_lo, *refs):
    weights, (own_ref, sums) = refs[:6], refs[6:]
    planes, third = own_ref.shape[0], sums.shape[1]
    for p in range(planes):
        taps = [a for a in range(3) if 0 <= p + a - 1 < planes]
        w_hi, w_lo = (jnp.concatenate([weights[2 * a + n][...] for a in taps], 0) for n in range(2))
        out = three_products(w_hi, w_lo, plane_of(g_hi, p), plane_of(g_lo, p))
        for n, a in enumerate(taps):
            q = p + a - 1
            part = out[n * third:(n + 1) * third]
            if p == max(q - 1, 0):
                sums[q] = part
            else:
                sums[q] += part
        if p:
            own_ref[p - 1] = spread(sums.at[p - 1])
    own_ref[planes - 1] = spread(sums.at[planes - 1])


def inner(halves, weights, planes, flops, name, flat=False):
    third = weights[0].shape[0]
    channels = third // len(SHIFTS)
    return call(flat_part if flat else inner_part, shape(planes, channels, AREA),
                [pltpu.VMEM((planes if flat else 2, third, AREA), F32)], [*halves, *weights], 0, flops, name)


def turned_kernel(spots, a, b, c, d, *refs):
    outs, turned = refs[:-1], refs[-1]
    turned[...] = (a[...] + b[...] + c[...] + d[...]).T
    height = outs[0].shape[0]
    for k, out in enumerate(outs):
        out[...] = turned[pl.ds(pl.multiple_of(spots[k] * height, height), height), :]


def turned_sum(spots, parts):
    rows, width = parts[0].shape
    return call(turned_kernel, [shape(width // 4, rows)] * 4, [pltpu.VMEM((width, rows), F32)],
                [spots, *parts], 1, name="turned_sum")


def last_kernel(scale, a, b, c, d, out):
    out[...] = ((a[...] + b[...] + c[...] + d[...]) * scale).T


def last_sum(parts, scale):
    height, rows = parts[0].shape
    return call(lambda *refs: last_kernel(scale, *refs), shape(rows, height), [], parts, name="last_sum")


def first_kernel(own, before, after, slope, out):
    planes = out.shape[0]
    for p in range(planes):
        value = own[p]
        if p == 0:
            value = value + before[0]
        if p == planes - 1:
            value = value + after[0]
        out[p] = value * slope[p]


def input_kernel(own, before, after, out):
    planes = own.shape[0]
    for p in range(planes):
        value = own[p]
        if p == 0:
            value = value + before[0]
        if p == planes - 1:
            value = value + after[0]
        out[p] = value


FAR = [(i, (i + 8) % 16) for i in range(16)]
TWIN = [(i, i ^ 1) for i in range(16)]
UP = [(i, i + 1) for i in range(SLABS - 1)]
DOWN = [(i + 1, i) for i in range(SLABS - 1)]


def along_x(d):
    return [(i, (i & 9) | ((i + 2 * d) & 6)) for i in range(16)]


def along_y(d):
    return [(i, (i + 4 * d) % 16) for i in range(16)]


def along_z(d):
    return [(i, (i & 12) | ((i + d) & 3)) for i in range(16)]


def send(value, moves, axis="chan"):
    return lax.ppermute(value, axis, moves)


def after(value, done):
    return lax.optimization_barrier((value, *done))[0]


def shard_ids():
    me = lax.axis_index("chan")
    row, far_row = ([s] + [(s & 9) | ((s - 2 * d) & 6) for d in (1, 3, 2)] for s in (me, me ^ 8))
    ids = row + far_row
    return jnp.stack(ids + [i ^ 1 for i in ids]).astype(jnp.int32)


def gathered(own, soon, late):
    far = send(own, FAR)
    near = [own] + [send(own, along_x(d)) for d in (1, 3, 2)]
    far = after(far, [*near[1:3], *soon])
    wide = [far] + [send(far, along_x(d)) for d in (1, 3, 2)]
    near_all = jnp.concatenate(near, 0)
    near_twin = send(near_all, TWIN)
    wide_all = jnp.concatenate(wide, 0)
    result, done = late(far, near_all, wide_all)
    wide_twin = send(after(wide_all, done), TWIN)
    return [*near, *wide, near_twin, wide_twin], result


def edges(before, after):
    return send(after, UP, "slab"), send(before, DOWN, "slab")


def to_row(part, d):
    return send(part, along_y(d), "slab")


def to_owners(rows):
    return [rows[0]] + [send(rows[d], along_z(d), "slab") for d in (1, 2, 3)]


def per_device(saved_input, pre_first, pre_second, out_grad, weight_first, weight_second):
    saved, pre1, pre2, grad = (jnp.transpose(v, (1, 0, 2)) for v in (saved_input, pre_first, pre_second, out_grad))
    planes, channels, area = saved.shape
    taps, _, total = weight_first.shape
    rows = taps * channels
    flops = 6 * rows * total * planes * area
    scale = 1.0 / math.sqrt(planes * SLABS * area)
    slab = lax.axis_index("slab")
    turn = ((slab // 4 + jnp.arange(4)) % 4).astype(jnp.int32)
    z_spots = ((slab + jnp.arange(4)) % 4).astype(jnp.int32)
    ids = shard_ids()
    spots = (((ids // 4 - slab // 4) % 4) * 4 + ids % 4).astype(jnp.int32)
    quarter = shape(rows, total // 4)
    second_grad = grad * slope_of(pre2)
    saved_rims = jnp.stack([saved[0], saved[planes - 1]])

    def second_weights_of(_, near, wide):
        return second_ready(after(turn, [wide]), weight_second, pre1, saved_rims), [saved_rims]

    pieces, (*w2, rims, slope) = gathered(second_grad, [], second_weights_of)

    n = len(pieces)
    halves, (before, behind) = first_use(
        lambda *refs: second_outer_kernel(n, *refs), spots, pieces, [rims, *w2[:2], *w2[4:]],
        [shape(3, channels, area)] * 2, flops // 9, "second_outer")
    before, behind = edges(before, behind)
    own = inner(halves, w2, planes, flops, "second_inner", True)
    first_grad = call(first_kernel, shape(planes, channels, area), [], [own, before, behind, slope], name="first_grad")
    h_hi, h_lo = input_halves(0, pre1, before, behind, "second_input")

    second_parts = filter_quarters(range(4), halves, (h_hi, h_lo), flops, "second_filter")

    def second_sum(far, near, _):
        parts = lax.optimization_barrier((*second_parts, near))[:4]
        one, three = to_row(parts[1], 1), to_row(parts[3], 3)
        two = to_row(after(parts[2], [one, three]), 2)
        halves = input_halves(1, after(saved, [far]), before, behind, "first_input")
        w1 = weight_halves(after(turn, [far]), weight_first, "first_weights")
        return ([parts[0], one, two, three], halves, w1), [one, three, *halves, *w1]

    pieces, (second_rows, inputs, w1) = gathered(first_grad, second_parts, second_sum)
    halves, (part_2, part_1) = first_use(
        lambda *refs: first_filter_kernel(n, (2, 1), *refs), spots, pieces, inputs, [quarter] * 2, flops // 2,
        "first_filter")
    row_2, row_1 = to_row(part_2, 2), to_row(part_1, 1)
    part_3, part_0 = filter_quarters((3, 0), halves, inputs, flops // 2, "first_filter_rest")
    first_rows = [part_0, row_1, row_2, to_row(part_3, 3)]

    second_rows = lax.optimization_barrier((*second_rows, part_0))[:4]
    second_rows = turned_sum(z_spots, second_rows)
    before, behind = call(first_outer_kernel, [shape(1, channels, area)] * 2, [],
                          [*halves, *w1[:2], *w1[4:]], 0, flops // 9, "first_outer")
    first_rows = lax.optimization_barrier((*first_rows, before))[:4]
    first_rows = turned_sum(z_spots, first_rows)
    own = inner([after(halves[0], [first_rows[0]]), halves[1]], w1, planes, flops, "first_inner")
    second_weights = last_sum(to_owners(second_rows), scale)
    first_weights = last_sum(to_owners(first_rows), scale)
    before, behind = edges(before, behind)
    input_grad = call(input_kernel, shape(planes, channels, area), [], [own, before, behind], name="input_grad")
    return (jnp.transpose(input_grad, (1, 0, 2)), first_weights.reshape(taps, channels, -1),
            second_weights.reshape(taps, channels, -1))


def solution(mesh):
    in_specs = (
        P("chan", "slab", None),
        P("chan", "slab", None),
        P("chan", "slab", None),
        P("chan", "slab", None),
        P(None, "chan", None),
        P(None, "chan", None),
    )
    out_specs = (P("chan", "slab", None), P(None, "chan", "slab"), P(None, "chan", "slab"))
    return jax.shard_map(
        per_device, mesh=mesh, in_specs=in_specs, out_specs=out_specs, check_vma=False
    )
```

```python
import math

import jax
import jax.numpy as jnp
from jax import lax
from jax.experimental import pallas as pl
from jax.experimental.pallas import tpu as pltpu
from jax.sharding import PartitionSpec as P

SIDE = 16
AREA = 256
SLABS = 16
SHIFTS = [(b, c) for b in (-1, 0, 1) for c in (-1, 0, 1)]
F32 = jnp.float32
BF16 = jnp.bfloat16
VM = pl.BlockSpec(memory_space=pltpu.VMEM)
SM = pl.BlockSpec(memory_space=pltpu.SMEM)


def slope_of(values):
    sigma = jax.nn.sigmoid(values)
    return sigma * (1.0 + values * (1.0 - sigma))


def call(kernel, out_shape, scratch, args, n_smem=0, flops=0, name=None):
    many = isinstance(out_shape, list)
    moved = sum(a.size * a.dtype.itemsize for a in args)
    moved += sum(o.size * o.dtype.itemsize for o in (out_shape if many else [out_shape]))
    return pl.pallas_call(
        kernel,
        out_shape=out_shape,
        in_specs=[SM] * n_smem + [VM] * (len(args) - n_smem),
        out_specs=[VM] * len(out_shape) if many else VM,
        scratch_shapes=scratch,
        compiler_params=pltpu.CompilerParams(vmem_limit_bytes=16 << 20),
        cost_estimate=pl.CostEstimate(flops=flops, bytes_accessed=moved, transcendentals=0),
        name=name,
    )(*args)


def shape(*dims, dtype=F32):
    return jax.ShapeDtypeStruct(dims, dtype)


def split(value):
    high = value.astype(BF16)
    return high, (value - high.astype(F32)).astype(BF16)


def moved_cells(plane, row_step, col_step):
    cells = lax.broadcasted_iota(jnp.int32, plane.shape, 1)
    if col_step:
        col = cells % SIDE + col_step
        plane = jnp.where((col >= 0) & (col < SIDE), pltpu.roll(plane, -col_step % AREA, 1), 0.0)
    if row_step:
        row = cells // SIDE + row_step
        plane = jnp.where((row >= 0) & (row < SIDE), pltpu.roll(plane, -row_step * SIDE % AREA, 1), 0.0)
    return plane


def weights_kernel(turn, source, *outs):
    taps, channels, total = source.shape
    width = total // 4
    for a in range(3):
        hi_ref, lo_ref = outs[2 * a:2 * a + 2]

        def one_tap(t, _):
            at = pl.ds(pl.multiple_of(t * channels, channels), channels)
            for d in range(4):
                lanes = pl.ds(pl.multiple_of(turn[d] * width, width), width)
                hi, lo = split(source[t + a * (taps // 3), :, lanes])
                hi_ref[at, d * width:(d + 1) * width] = hi
                lo_ref[at, d * width:(d + 1) * width] = lo
            return 0

        lax.fori_loop(0, taps // 3, one_tap, 0)


def weight_halves(turn, weight, name):
    taps, channels, total = weight.shape
    flat = shape(taps // 3 * channels, total, dtype=BF16)
    return call(weights_kernel, [flat] * 6, [], [turn, weight], 1, name=name)


def second_kernel(turn, source, pre, saved, *outs):
    *halves, rims, slope = outs
    for n, p in enumerate((0, slope.shape[0] - 1)):
        rims[n, 0] = pre[p]
        rims[n, 1] = saved[n]
    slope[...] = slope_of(pre[...])
    weights_kernel(turn, source, *halves)


def second_ready(turn, weight, pre, saved):
    taps, channels, total = weight.shape
    outs = [shape(taps // 3 * channels, total, dtype=BF16)] * 6 + [shape(2, 2, *pre.shape[1:]), shape(*pre.shape)]
    return call(second_kernel, outs, [], [turn, weight, pre, saved], 1, name="second_ready")


def inputs_kernel(n, own_ref, low_ref, high_ref, hi_ref, lo_ref, rows):
    planes, channels, _ = own_ref.shape
    rows[0] = low_ref[n + 1]
    rows[planes + 1] = high_ref[n + 1]
    rows[1:planes + 1] = own_ref[...]

    def one_plane(q, _):
        plane = rows[q]
        if n == 0:
            plane = plane * jax.nn.sigmoid(plane)
        lanes = pl.ds(pl.multiple_of(q * AREA, AREA), AREA)
        for s, (b, c) in enumerate(SHIFTS):
            hi, lo = split(moved_cells(plane, b, c))
            hi_ref[s * channels:(s + 1) * channels, lanes] = hi
            lo_ref[s * channels:(s + 1) * channels, lanes] = lo
        return 0

    lax.fori_loop(0, planes + 2, one_plane, 0)


def input_halves(n, own, low, high, name):
    planes, channels, area = own.shape
    tall = shape(len(SHIFTS) * channels, (planes + 2) * area, dtype=BF16)
    return call(lambda *refs: inputs_kernel(n, *refs), [tall] * 2, [pltpu.VMEM((planes + 2, channels, area), F32)],
                [own, low, high], name=name)


def lanes_of(p):
    return pl.ds(p * AREA if isinstance(p, int) else pl.multiple_of(p * AREA, AREA), AREA)


def split_plane(spots, pieces, p, planes, g_hi, g_lo):
    k = 0
    for piece in pieces:
        for first in range(0, piece.shape[0], planes):
            hi, lo = split(piece[first + p])
            g_hi[spots[k], :, lanes_of(p)] = hi
            g_lo[spots[k], :, lanes_of(p)] = lo
            k += 1


def spread(sums):
    channels = sums.shape[0] // len(SHIFTS)
    total = jnp.zeros((channels, AREA), F32)
    for b in (-1, 0, 1):
        row = jnp.zeros((channels, AREA), F32)
        for c in (-1, 0, 1):
            s = SHIFTS.index((b, c)) * channels
            row += moved_cells(sums[s:s + channels, :], 0, -c)
        total += moved_cells(row, -b, 0)
    return total


def three_products(w_hi, w_lo, hi, lo):
    out = jnp.dot(w_hi, hi, preferred_element_type=F32)
    out += jnp.dot(w_hi, lo, preferred_element_type=F32)
    return out + jnp.dot(w_lo, hi, preferred_element_type=F32)


def plane_of(g_ref, p):
    return g_ref[:, :, lanes_of(p)].reshape(g_ref.shape[0] * g_ref.shape[1], AREA)


def outer_part(first, last, w_refs, before_ref, behind_ref, rims=None):
    for n, (planes, w_hi, w_lo, out) in enumerate(((first, *w_refs[:2], before_ref), (last, *w_refs[2:], behind_ref))):
        out[0] = spread(three_products(w_hi[...], w_lo[...], *planes))
        if rims is not None:
            out[1:] = rims[n]


def second_outer_kernel(n, spots, *refs):
    pieces, rims, weights, (g_hi, g_lo, before_ref, behind_ref) = refs[:n], refs[n], refs[n + 1:n + 5], refs[n + 5:]
    last = g_hi.shape[2] // AREA - 1
    split_plane(spots, pieces, 0, last + 1, g_hi, g_lo)
    split_plane(spots, pieces, last, last + 1, g_hi, g_lo)
    outer_part(*([plane_of(g, p) for g in (g_hi, g_lo)] for p in (0, last)), weights, before_ref, behind_ref, rims)
    for p in range(1, last):
        split_plane(spots, pieces, p, last + 1, g_hi, g_lo)


def first_outer_kernel(g_hi, g_lo, *refs):
    last = g_hi.shape[2] // AREA - 1
    outer_part(*([plane_of(g, p) for g in (g_hi, g_lo)] for p in (0, last)), refs[:4], *refs[4:])


def inner_part(g_hi, g_lo, *refs):
    weights, (own_ref, sums) = refs[:6], refs[6:]
    planes = own_ref.shape[0]

    def add_up(q, taps):
        total = None
        for a in taps:
            out = three_products(weights[2 * a][...], weights[2 * a + 1][...],
                                 plane_of(g_hi, q + 1 - a), plane_of(g_lo, q + 1 - a))
            total = out if total is None else total + out
        sums[q % 2] = total

    def one_plane(q, _):
        add_up(q, (0, 1, 2))
        own_ref[q - 1] = spread(sums.at[(q - 1) % 2])
        return 0

    add_up(0, (0, 1))
    lax.fori_loop(1, planes - 1, one_plane, 0)
    add_up(planes - 1, (1, 2))
    own_ref[planes - 2] = spread(sums.at[(planes - 2) % 2])
    own_ref[planes - 1] = spread(sums.at[(planes - 1) % 2])


def filter_add(p, hi, lo, i_hi, i_lo, outs):
    width = outs[0].shape[1]
    left_hi, left_lo = (jnp.concatenate([i[:, lanes_of(p + a)] for a in range(3)], 0) for i in (i_hi, i_lo))
    dims = (((1,), (1,)), ((), ()))
    part = lax.dot_general(left_hi, hi, dims, preferred_element_type=F32)
    part += lax.dot_general(left_hi, lo, dims, preferred_element_type=F32)
    part += lax.dot_general(left_lo, hi, dims, preferred_element_type=F32)
    for n, out in enumerate(outs):
        out[...] += part[:, n * width:(n + 1) * width]


def quarters_of(g_ref, p, quarters):
    blocks = g_ref.shape[0] // 4
    width = blocks * g_ref.shape[1]
    return jnp.concatenate([g_ref[d * blocks:(d + 1) * blocks, :, lanes_of(p)].reshape(width, AREA) for d in quarters], 0)


def filter_kernel(quarters, g_hi, g_lo, i_hi, i_lo, *outs):
    for out in outs:
        out[...] = jnp.zeros_like(out)

    for p in range(g_hi.shape[2] // AREA):
        filter_add(p, quarters_of(g_hi, p, quarters), quarters_of(g_lo, p, quarters), i_hi, i_lo, outs)


def filter_quarters(quarters, halves, inputs, flops, name):
    rows, total = 3 * inputs[0].shape[0], halves[0].shape[0] * halves[0].shape[1]
    return call(lambda *refs: filter_kernel(quarters, *refs), [shape(rows, total // 4)] * len(quarters), [],
                [*halves, *inputs], 0, flops, name)


def first_filter_kernel(n, quarters, spots, *refs):
    pieces, inputs, (g_hi, g_lo), outs = refs[:n], refs[n:n + 2], refs[n + 2:n + 4], refs[n + 4:n + 4 + len(quarters)]
    planes = g_hi.shape[2] // AREA
    for out in outs:
        out[...] = jnp.zeros_like(out)
    split_plane(spots, pieces, 0, planes, g_hi, g_lo)
    for p in range(planes):
        filter_add(p, quarters_of(g_hi, p, quarters), quarters_of(g_lo, p, quarters), *inputs, outs)
        if p + 1 < planes:
            split_plane(spots, pieces, p + 1, planes, g_hi, g_lo)


def first_use(kernel, spots, pieces, others, outs, flops, name):
    planes, channels, area = pieces[0].shape
    shards = sum(piece.shape[0] for piece in pieces) // planes
    halves = [shape(shards, channels, planes * area, dtype=BF16)] * 2
    g_hi, g_lo, *rest = call(kernel, halves + outs, [], [spots, *pieces, *others], 1, flops, name)
    return (g_hi, g_lo), rest


def flat_part(g_hi, g_lo, *refs):
    weights, (own_ref, sums) = refs[:6], refs[6:]
    planes, third = own_ref.shape[0], sums.shape[1]
    for p in range(planes):
        taps = [a for a in range(3) if 0 <= p + a - 1 < planes]
        w_hi, w_lo = (jnp.concatenate([weights[2 * a + n][...] for a in taps], 0) for n in range(2))
        out = three_products(w_hi, w_lo, plane_of(g_hi, p), plane_of(g_lo, p))
        for n, a in enumerate(taps):
            q = p + a - 1
            part = out[n * third:(n + 1) * third]
            if p == max(q - 1, 0):
                sums[q] = part
            else:
                sums[q] += part
        if p:
            own_ref[p - 1] = spread(sums.at[p - 1])
    own_ref[planes - 1] = spread(sums.at[planes - 1])


def inner(halves, weights, planes, flops, name, flat=False):
    third = weights[0].shape[0]
    channels = third // len(SHIFTS)
    return call(flat_part if flat else inner_part, shape(planes, channels, AREA),
                [pltpu.VMEM((planes if flat else 2, third, AREA), F32)], [*halves, *weights], 0, flops, name)


def turned_kernel(spots, a, b, c, d, *refs):
    outs, turned = refs[:-1], refs[-1]
    turned[...] = (a[...] + b[...] + c[...] + d[...]).T
    height = outs[0].shape[0]
    for k, out in enumerate(outs):
        out[...] = turned[pl.ds(pl.multiple_of(spots[k] * height, height), height), :]


def turned_sum(spots, parts):
    rows, width = parts[0].shape
    return call(turned_kernel, [shape(width // 4, rows)] * 4, [pltpu.VMEM((width, rows), F32)],
                [spots, *parts], 1, name="turned_sum")


def last_kernel(scale, a, b, c, d, out):
    out[...] = ((a[...] + b[...] + c[...] + d[...]) * scale).T


def last_sum(parts, scale):
    height, rows = parts[0].shape
    return call(lambda *refs: last_kernel(scale, *refs), shape(rows, height), [], parts, name="last_sum")


def first_kernel(own, before, after, slope, out):
    planes = out.shape[0]
    for p in range(planes):
        value = own[p]
        if p == 0:
            value = value + before[0]
        if p == planes - 1:
            value = value + after[0]
        out[p] = value * slope[p]


def input_kernel(own, before, after, out):
    planes = own.shape[0]
    for p in range(planes):
        value = own[p]
        if p == 0:
            value = value + before[0]
        if p == planes - 1:
            value = value + after[0]
        out[p] = value


FAR = [(i, (i + 8) % 16) for i in range(16)]
TWIN = [(i, i ^ 1) for i in range(16)]
UP = [(i, i + 1) for i in range(SLABS - 1)]
DOWN = [(i + 1, i) for i in range(SLABS - 1)]


def along_x(d):
    return [(i, (i & 9) | ((i + 2 * d) & 6)) for i in range(16)]


def along_y(d):
    return [(i, (i + 4 * d) % 16) for i in range(16)]


def along_z(d):
    return [(i, (i & 12) | ((i + d) & 3)) for i in range(16)]


def send(value, moves, axis="chan"):
    return lax.ppermute(value, axis, moves)


def after(value, done):
    return lax.optimization_barrier((value, *done))[0]


def shard_ids():
    me = lax.axis_index("chan")
    row, far_row = ([s] + [(s & 9) | ((s - 2 * d) & 6) for d in (1, 3, 2)] for s in (me, me ^ 8))
    ids = row + far_row
    return jnp.stack(ids + [i ^ 1 for i in ids]).astype(jnp.int32)


def gathered(own, soon, late):
    far = send(own, FAR)
    near = [own] + [send(own, along_x(d)) for d in (1, 3, 2)]
    far = after(far, [*near[1:3], *soon])
    wide = [far] + [send(far, along_x(d)) for d in (1, 3, 2)]
    near_all = jnp.concatenate(near, 0)
    near_twin = send(near_all, TWIN)
    wide_all = jnp.concatenate(wide, 0)
    result, done = late(far, near_all, wide_all)
    wide_twin = send(after(wide_all, done), TWIN)
    return [*near, *wide, near_twin, wide_twin], result


def edges(before, after):
    return send(after, UP, "slab"), send(before, DOWN, "slab")


def to_row(part, d):
    return send(part, along_y(d), "slab")


def to_owners(rows):
    return [rows[0]] + [send(rows[d], along_z(d), "slab") for d in (1, 2, 3)]


def per_device(saved_input, pre_first, pre_second, out_grad, weight_first, weight_second):
    saved, pre1, pre2, grad = (jnp.transpose(v, (1, 0, 2)) for v in (saved_input, pre_first, pre_second, out_grad))
    planes, channels, area = saved.shape
    taps, _, total = weight_first.shape
    rows = taps * channels
    flops = 6 * rows * total * planes * area
    scale = 1.0 / math.sqrt(planes * SLABS * area)
    slab = lax.axis_index("slab")
    turn = ((slab // 4 + jnp.arange(4)) % 4).astype(jnp.int32)
    z_spots = ((slab + jnp.arange(4)) % 4).astype(jnp.int32)
    ids = shard_ids()
    spots = (((ids // 4 - slab // 4) % 4) * 4 + ids % 4).astype(jnp.int32)
    quarter = shape(rows, total // 4)
    second_grad = grad * slope_of(pre2)
    saved_rims = jnp.stack([saved[0], saved[planes - 1]])

    def second_weights_of(_, near, wide):
        return second_ready(after(turn, [wide]), weight_second, pre1, saved_rims), [saved_rims]

    pieces, (*w2, rims, slope) = gathered(second_grad, [], second_weights_of)

    n = len(pieces)
    halves, (before, behind) = first_use(
        lambda *refs: second_outer_kernel(n, *refs), spots, pieces, [rims, *w2[:2], *w2[4:]],
        [shape(3, channels, area)] * 2, flops // 9, "second_outer")
    before, behind = edges(before, behind)
    own = inner(halves, w2, planes, flops, "second_inner", True)
    first_grad = call(first_kernel, shape(planes, channels, area), [], [own, before, behind, slope], name="first_grad")
    h_hi, h_lo = input_halves(0, pre1, before, behind, "second_input")

    second_parts = filter_quarters(range(4), halves, (h_hi, h_lo), flops, "second_filter")

    def second_sum(far, near, _):
        parts = lax.optimization_barrier((*second_parts, near))[:4]
        one, three = to_row(parts[1], 1), to_row(parts[3], 3)
        two = to_row(after(parts[2], [one, three]), 2)
        halves = input_halves(1, after(saved, [far]), before, behind, "first_input")
        w1 = weight_halves(after(turn, [far]), weight_first, "first_weights")
        return ([parts[0], one, two, three], halves, w1), [one, three, *halves, *w1]

    pieces, (second_rows, inputs, w1) = gathered(first_grad, second_parts, second_sum)
    halves, (part_2, part_1) = first_use(
        lambda *refs: first_filter_kernel(n, (2, 1), *refs), spots, pieces, inputs, [quarter] * 2, flops // 2,
        "first_filter")
    row_2, row_1 = to_row(part_2, 2), to_row(part_1, 1)
    part_3, part_0 = filter_quarters((3, 0), halves, inputs, flops // 2, "first_filter_rest")
    first_rows = [part_0, row_1, row_2, to_row(part_3, 3)]

    before, behind = call(first_outer_kernel, [shape(1, channels, area)] * 2, [],
                          [after(halves[0], [part_0]), halves[1], *w1[:2], *w1[4:]], 0, flops // 9, "first_outer")
    before, behind = edges(before, behind)
    second_rows = lax.optimization_barrier((*second_rows, part_0, before, behind))[:4]
    second_rows = turned_sum(z_spots, second_rows)
    first_rows = lax.optimization_barrier((*first_rows, second_rows[0]))[:4]
    first_rows = turned_sum(z_spots, first_rows)
    own = inner([after(halves[0], [first_rows[0]]), halves[1]], w1, planes, flops, "first_inner", True)
    second_rows = lax.optimization_barrier((*to_owners(second_rows), first_rows[0]))[:4]
    second_weights = last_sum(second_rows, scale)
    first_weights = last_sum(to_owners(first_rows), scale)
    input_grad = call(input_kernel, shape(planes, channels, area), [], [own, before, behind], name="input_grad")
    return (jnp.transpose(input_grad, (1, 0, 2)), first_weights.reshape(taps, channels, -1),
            second_weights.reshape(taps, channels, -1))


def solution(mesh):
    in_specs = (
        P("chan", "slab", None),
        P("chan", "slab", None),
        P("chan", "slab", None),
        P("chan", "slab", None),
        P(None, "chan", None),
        P(None, "chan", None),
    )
    out_specs = (P("chan", "slab", None), P(None, "chan", "slab"), P(None, "chan", "slab"))
    return jax.shard_map(
        per_device, mesh=mesh, in_specs=in_specs, out_specs=out_specs, check_vma=False
    )
```

```python
import math

import jax
import jax.numpy as jnp
from jax import lax
from jax.experimental import pallas as pl
from jax.experimental.pallas import tpu as pltpu
from jax.sharding import PartitionSpec as P

SIDE = 16
AREA = 256
SLABS = 16
SHIFTS = [(b, c) for b in (-1, 0, 1) for c in (-1, 0, 1)]
F32 = jnp.float32
BF16 = jnp.bfloat16
VM = pl.BlockSpec(memory_space=pltpu.VMEM)
SM = pl.BlockSpec(memory_space=pltpu.SMEM)


def slope_of(values):
    sigma = jax.nn.sigmoid(values)
    return sigma * (1.0 + values * (1.0 - sigma))


def call(kernel, out_shape, scratch, args, n_smem=0, flops=0, name=None):
    many = isinstance(out_shape, list)
    moved = sum(a.size * a.dtype.itemsize for a in args)
    moved += sum(o.size * o.dtype.itemsize for o in (out_shape if many else [out_shape]))
    return pl.pallas_call(
        kernel,
        out_shape=out_shape,
        in_specs=[SM] * n_smem + [VM] * (len(args) - n_smem),
        out_specs=[VM] * len(out_shape) if many else VM,
        scratch_shapes=scratch,
        compiler_params=pltpu.CompilerParams(vmem_limit_bytes=16 << 20),
        cost_estimate=pl.CostEstimate(flops=flops, bytes_accessed=moved, transcendentals=0),
        name=name,
    )(*args)


def shape(*dims, dtype=F32):
    return jax.ShapeDtypeStruct(dims, dtype)


def split(value):
    high = value.astype(BF16)
    return high, (value - high.astype(F32)).astype(BF16)


def moved_cells(plane, row_step, col_step):
    cells = lax.broadcasted_iota(jnp.int32, plane.shape, 1)
    if col_step:
        col = cells % SIDE + col_step
        plane = jnp.where((col >= 0) & (col < SIDE), pltpu.roll(plane, -col_step % AREA, 1), 0.0)
    if row_step:
        row = cells // SIDE + row_step
        plane = jnp.where((row >= 0) & (row < SIDE), pltpu.roll(plane, -row_step * SIDE % AREA, 1), 0.0)
    return plane


def weights_kernel(turn, source, *outs):
    taps, channels, total = source.shape
    width = total // 4
    for a in range(3):
        hi_ref, lo_ref = outs[2 * a:2 * a + 2]

        def one_tap(t, _):
            at = pl.ds(pl.multiple_of(t * channels, channels), channels)
            for d in range(4):
                lanes = pl.ds(pl.multiple_of(turn[d] * width, width), width)
                hi, lo = split(source[t + a * (taps // 3), :, lanes])
                hi_ref[at, d * width:(d + 1) * width] = hi
                lo_ref[at, d * width:(d + 1) * width] = lo
            return 0

        lax.fori_loop(0, taps // 3, one_tap, 0)


def weight_halves(turn, weight, name):
    taps, channels, total = weight.shape
    flat = shape(taps // 3 * channels, total, dtype=BF16)
    return call(weights_kernel, [flat] * 6, [], [turn, weight], 1, name=name)


def second_kernel(turn, source, pre, saved, *outs):
    *halves, rims, slope = outs
    for n, p in enumerate((0, slope.shape[0] - 1)):
        rims[n, 0] = pre[p]
        rims[n, 1] = saved[n]
    slope[...] = slope_of(pre[...])
    weights_kernel(turn, source, *halves)


def second_ready(turn, weight, pre, saved):
    taps, channels, total = weight.shape
    outs = [shape(taps // 3 * channels, total, dtype=BF16)] * 6 + [shape(2, 2, *pre.shape[1:]), shape(*pre.shape)]
    return call(second_kernel, outs, [], [turn, weight, pre, saved], 1, name="second_ready")


def inputs_kernel(n, own_ref, low_ref, high_ref, hi_ref, lo_ref, rows):
    planes, channels, _ = own_ref.shape
    rows[0] = low_ref[n + 1]
    rows[planes + 1] = high_ref[n + 1]
    rows[1:planes + 1] = own_ref[...]

    def one_plane(q, _):
        plane = rows[q]
        if n == 0:
            plane = plane * jax.nn.sigmoid(plane)
        lanes = pl.ds(pl.multiple_of(q * AREA, AREA), AREA)
        for s, (b, c) in enumerate(SHIFTS):
            hi, lo = split(moved_cells(plane, b, c))
            hi_ref[s * channels:(s + 1) * channels, lanes] = hi
            lo_ref[s * channels:(s + 1) * channels, lanes] = lo
        return 0

    lax.fori_loop(0, planes + 2, one_plane, 0)


def input_halves(n, own, low, high, name):
    planes, channels, area = own.shape
    tall = shape(len(SHIFTS) * channels, (planes + 2) * area, dtype=BF16)
    return call(lambda *refs: inputs_kernel(n, *refs), [tall] * 2, [pltpu.VMEM((planes + 2, channels, area), F32)],
                [own, low, high], name=name)


def lanes_of(p):
    return pl.ds(p * AREA if isinstance(p, int) else pl.multiple_of(p * AREA, AREA), AREA)


def split_plane(spots, pieces, p, planes, g_hi, g_lo):
    k = 0
    for piece in pieces:
        for first in range(0, piece.shape[0], planes):
            hi, lo = split(piece[first + p])
            g_hi[spots[k], :, lanes_of(p)] = hi
            g_lo[spots[k], :, lanes_of(p)] = lo
            k += 1


def spread(sums):
    channels = sums.shape[0] // len(SHIFTS)
    total = jnp.zeros((channels, AREA), F32)
    for b in (-1, 0, 1):
        row = jnp.zeros((channels, AREA), F32)
        for c in (-1, 0, 1):
            s = SHIFTS.index((b, c)) * channels
            row += moved_cells(sums[s:s + channels, :], 0, -c)
        total += moved_cells(row, -b, 0)
    return total


def three_products(w_hi, w_lo, hi, lo):
    out = jnp.dot(w_hi, hi, preferred_element_type=F32)
    out += jnp.dot(w_hi, lo, preferred_element_type=F32)
    return out + jnp.dot(w_lo, hi, preferred_element_type=F32)


def plane_of(g_ref, p):
    return g_ref[:, :, lanes_of(p)].reshape(g_ref.shape[0] * g_ref.shape[1], AREA)


def outer_part(first, last, w_refs, before_ref, behind_ref, rims=None):
    for n, (planes, w_hi, w_lo, out) in enumerate(((first, *w_refs[:2], before_ref), (last, *w_refs[2:], behind_ref))):
        out[0] = spread(three_products(w_hi[...], w_lo[...], *planes))
        if rims is not None:
            out[1:] = rims[n]


def second_outer_kernel(n, spots, *refs):
    pieces, rims, weights, (g_hi, g_lo, before_ref, behind_ref) = refs[:n], refs[n], refs[n + 1:n + 5], refs[n + 5:]
    last = g_hi.shape[2] // AREA - 1
    split_plane(spots, pieces, 0, last + 1, g_hi, g_lo)
    split_plane(spots, pieces, last, last + 1, g_hi, g_lo)
    outer_part(*([plane_of(g, p) for g in (g_hi, g_lo)] for p in (0, last)), weights, before_ref, behind_ref, rims)
    for p in range(1, last):
        split_plane(spots, pieces, p, last + 1, g_hi, g_lo)


def first_outer_kernel(g_hi, g_lo, *refs):
    last = g_hi.shape[2] // AREA - 1
    outer_part(*([plane_of(g, p) for g in (g_hi, g_lo)] for p in (0, last)), refs[:4], *refs[4:])


def inner_part(g_hi, g_lo, *refs):
    weights, (own_ref, sums) = refs[:6], refs[6:]
    planes = own_ref.shape[0]

    def add_up(q, taps):
        total = None
        for a in taps:
            out = three_products(weights[2 * a][...], weights[2 * a + 1][...],
                                 plane_of(g_hi, q + 1 - a), plane_of(g_lo, q + 1 - a))
            total = out if total is None else total + out
        sums[q % 2] = total

    def one_plane(q, _):
        add_up(q, (0, 1, 2))
        own_ref[q - 1] = spread(sums.at[(q - 1) % 2])
        return 0

    add_up(0, (0, 1))
    lax.fori_loop(1, planes - 1, one_plane, 0)
    add_up(planes - 1, (1, 2))
    own_ref[planes - 2] = spread(sums.at[(planes - 2) % 2])
    own_ref[planes - 1] = spread(sums.at[(planes - 1) % 2])


def filter_add(p, hi, lo, i_hi, i_lo, outs):
    width = outs[0].shape[1]
    left_hi, left_lo = (jnp.concatenate([i[:, lanes_of(p + a)] for a in range(3)], 0) for i in (i_hi, i_lo))
    dims = (((1,), (1,)), ((), ()))
    part = lax.dot_general(left_hi, hi, dims, preferred_element_type=F32)
    part += lax.dot_general(left_hi, lo, dims, preferred_element_type=F32)
    part += lax.dot_general(left_lo, hi, dims, preferred_element_type=F32)
    for n, out in enumerate(outs):
        out[...] += part[:, n * width:(n + 1) * width]


def quarters_of(g_ref, p, quarters):
    blocks = g_ref.shape[0] // 4
    width = blocks * g_ref.shape[1]
    return jnp.concatenate([g_ref[d * blocks:(d + 1) * blocks, :, lanes_of(p)].reshape(width, AREA) for d in quarters], 0)


def filter_kernel(quarters, g_hi, g_lo, i_hi, i_lo, *outs):
    for out in outs:
        out[...] = jnp.zeros_like(out)

    for p in range(g_hi.shape[2] // AREA):
        filter_add(p, quarters_of(g_hi, p, quarters), quarters_of(g_lo, p, quarters), i_hi, i_lo, outs)


def filter_quarters(quarters, halves, inputs, flops, name):
    rows, total = 3 * inputs[0].shape[0], halves[0].shape[0] * halves[0].shape[1]
    return call(lambda *refs: filter_kernel(quarters, *refs), [shape(rows, total // 4)] * len(quarters), [],
                [*halves, *inputs], 0, flops, name)


def first_filter_kernel(n, quarters, spots, *refs):
    pieces, inputs, (g_hi, g_lo), outs = refs[:n], refs[n:n + 2], refs[n + 2:n + 4], refs[n + 4:n + 4 + len(quarters)]
    planes = g_hi.shape[2] // AREA
    for out in outs:
        out[...] = jnp.zeros_like(out)
    split_plane(spots, pieces, 0, planes, g_hi, g_lo)
    for p in range(planes):
        filter_add(p, quarters_of(g_hi, p, quarters), quarters_of(g_lo, p, quarters), *inputs, outs)
        if p + 1 < planes:
            split_plane(spots, pieces, p + 1, planes, g_hi, g_lo)


def first_use(kernel, spots, pieces, others, outs, flops, name):
    planes, channels, area = pieces[0].shape
    shards = sum(piece.shape[0] for piece in pieces) // planes
    halves = [shape(shards, channels, planes * area, dtype=BF16)] * 2
    g_hi, g_lo, *rest = call(kernel, halves + outs, [], [spots, *pieces, *others], 1, flops, name)
    return (g_hi, g_lo), rest


def flat_part(g_hi, g_lo, *refs):
    weights, (own_ref, sums) = refs[:6], refs[6:]
    planes, third = own_ref.shape[0], sums.shape[1]
    for p in range(planes):
        taps = [a for a in range(3) if 0 <= p + a - 1 < planes]
        w_hi, w_lo = (jnp.concatenate([weights[2 * a + n][...] for a in taps], 0) for n in range(2))
        out = three_products(w_hi, w_lo, plane_of(g_hi, p), plane_of(g_lo, p))
        for n, a in enumerate(taps):
            q = p + a - 1
            part = out[n * third:(n + 1) * third]
            if p == max(q - 1, 0):
                sums[q] = part
            else:
                sums[q] += part
        if p:
            own_ref[p - 1] = spread(sums.at[p - 1])
    own_ref[planes - 1] = spread(sums.at[planes - 1])


def inner(halves, weights, planes, flops, name, flat=False):
    third = weights[0].shape[0]
    channels = third // len(SHIFTS)
    return call(flat_part if flat else inner_part, shape(planes, channels, AREA),
                [pltpu.VMEM((planes if flat else 2, third, AREA), F32)], [*halves, *weights], 0, flops, name)


def turned_kernel(spots, a, b, c, d, *refs):
    outs, turned = refs[:-1], refs[-1]
    turned[...] = (a[...] + b[...] + c[...] + d[...]).T
    height = outs[0].shape[0]
    for k, out in enumerate(outs):
        out[...] = turned[pl.ds(pl.multiple_of(spots[k] * height, height), height), :]


def turned_sum(spots, parts):
    rows, width = parts[0].shape
    return call(turned_kernel, [shape(width // 4, rows)] * 4, [pltpu.VMEM((width, rows), F32)],
                [spots, *parts], 1, name="turned_sum")


def last_kernel(scale, a, b, c, d, out):
    out[...] = ((a[...] + b[...] + c[...] + d[...]) * scale).T


def last_sum(parts, scale):
    height, rows = parts[0].shape
    return call(lambda *refs: last_kernel(scale, *refs), shape(rows, height), [], parts, name="last_sum")


def first_kernel(own, before, after, slope, out):
    planes = out.shape[0]
    for p in range(planes):
        value = own[p]
        if p == 0:
            value = value + before[0]
        if p == planes - 1:
            value = value + after[0]
        out[p] = value * slope[p]


def input_kernel(own, before, after, out):
    planes = own.shape[0]
    for p in range(planes):
        value = own[p]
        if p == 0:
            value = value + before[0]
        if p == planes - 1:
            value = value + after[0]
        out[p] = value


FAR = [(i, (i + 8) % 16) for i in range(16)]
TWIN = [(i, i ^ 1) for i in range(16)]
UP = [(i, i + 1) for i in range(SLABS - 1)]
DOWN = [(i + 1, i) for i in range(SLABS - 1)]


def along_x(d):
    return [(i, (i & 9) | ((i + 2 * d) & 6)) for i in range(16)]


def along_y(d):
    return [(i, (i + 4 * d) % 16) for i in range(16)]


def along_z(d):
    return [(i, (i & 12) | ((i + d) & 3)) for i in range(16)]


def send(value, moves, axis="chan"):
    return lax.ppermute(value, axis, moves)


def after(value, done):
    return lax.optimization_barrier((value, *done))[0]


def shard_ids():
    me = lax.axis_index("chan")
    row, far_row = ([s] + [(s & 9) | ((s - 2 * d) & 6) for d in (1, 3, 2)] for s in (me, me ^ 8))
    ids = row + far_row
    return jnp.stack(ids + [i ^ 1 for i in ids]).astype(jnp.int32)


def gathered(own, soon, late):
    far = send(own, FAR)
    near = [own] + [send(own, along_x(d)) for d in (1, 3, 2)]
    far = after(far, [*near[1:3], *soon])
    wide = [far] + [send(far, along_x(d)) for d in (1, 3, 2)]
    near_all = jnp.concatenate(near, 0)
    near_twin = send(near_all, TWIN)
    wide_all = jnp.concatenate(wide, 0)
    result, done = late(far, near_all, wide_all)
    wide_twin = send(after(wide_all, done), TWIN)
    return [*near, *wide, near_twin, wide_twin], result


def edges(before, after):
    return send(after, UP, "slab"), send(before, DOWN, "slab")


def to_row(part, d):
    return send(part, along_y(d), "slab")


def to_owners(rows):
    return [rows[0]] + [send(rows[d], along_z(d), "slab") for d in (1, 2, 3)]


def per_device(saved_input, pre_first, pre_second, out_grad, weight_first, weight_second):
    saved, pre1, pre2, grad = (jnp.transpose(v, (1, 0, 2)) for v in (saved_input, pre_first, pre_second, out_grad))
    planes, channels, area = saved.shape
    taps, _, total = weight_first.shape
    rows = taps * channels
    flops = 6 * rows * total * planes * area
    scale = 1.0 / math.sqrt(planes * SLABS * area)
    slab = lax.axis_index("slab")
    turn = ((slab // 4 + jnp.arange(4)) % 4).astype(jnp.int32)
    z_spots = ((slab + jnp.arange(4)) % 4).astype(jnp.int32)
    ids = shard_ids()
    spots = (((ids // 4 - slab // 4) % 4) * 4 + ids % 4).astype(jnp.int32)
    quarter = shape(rows, total // 4)
    second_grad = grad * slope_of(pre2)
    saved_rims = jnp.stack([saved[0], saved[planes - 1]])

    def second_weights_of(_, near, wide):
        return second_ready(after(turn, [wide]), weight_second, pre1, saved_rims), [saved_rims]

    pieces, (*w2, rims, slope) = gathered(second_grad, [], second_weights_of)

    n = len(pieces)
    halves, (before, behind) = first_use(
        lambda *refs: second_outer_kernel(n, *refs), spots, pieces, [rims, *w2[:2], *w2[4:]],
        [shape(3, channels, area)] * 2, flops // 9, "second_outer")
    before, behind = edges(before, behind)
    own = inner(halves, w2, planes, flops, "second_inner", True)
    first_grad = call(first_kernel, shape(planes, channels, area), [], [own, before, behind, slope], name="first_grad")
    h_hi, h_lo = input_halves(0, pre1, before, behind, "second_input")

    second_parts = filter_quarters(range(4), halves, (h_hi, h_lo), flops, "second_filter")

    def second_sum(far, near, _):
        parts = lax.optimization_barrier((*second_parts, near))[:4]
        two = to_row(parts[2], 2)
        one, three = to_row(after(parts[1], [two]), 1), to_row(after(parts[3], [two]), 3)
        halves = input_halves(1, after(saved, [far]), before, behind, "first_input")
        w1 = weight_halves(after(turn, [far]), weight_first, "first_weights")
        return ([parts[0], one, two, three], halves, w1), [two, *halves, *w1]

    pieces, (second_rows, inputs, w1) = gathered(first_grad, second_parts, second_sum)
    halves, (part_2, part_1) = first_use(
        lambda *refs: first_filter_kernel(n, (2, 1), *refs), spots, pieces, inputs, [quarter] * 2, flops // 2,
        "first_filter")
    row_2, row_1 = to_row(part_2, 2), to_row(part_1, 1)
    part_3, part_0 = filter_quarters((3, 0), halves, inputs, flops // 2, "first_filter_rest")
    first_rows = [part_0, row_1, row_2, to_row(part_3, 3)]

    before, behind = call(first_outer_kernel, [shape(1, channels, area)] * 2, [],
                          [after(halves[0], [part_0]), halves[1], *w1[:2], *w1[4:]], 0, flops // 9, "first_outer")
    before, behind = edges(before, behind)
    second_rows = lax.optimization_barrier((*second_rows, part_0, before, behind))[:4]
    second_rows = turned_sum(z_spots, second_rows)
    first_rows = lax.optimization_barrier((*first_rows, second_rows[0]))[:4]
    first_rows = turned_sum(z_spots, first_rows)
    own = inner([after(halves[0], [first_rows[0]]), halves[1]], w1, planes, flops, "first_inner", True)
    second_rows = lax.optimization_barrier((*to_owners(second_rows), first_rows[0]))[:4]
    second_weights = last_sum(second_rows, scale)
    first_weights = last_sum(to_owners(first_rows), scale)
    input_grad = call(input_kernel, shape(planes, channels, area), [], [own, before, behind], name="input_grad")
    return (jnp.transpose(input_grad, (1, 0, 2)), first_weights.reshape(taps, channels, -1),
            second_weights.reshape(taps, channels, -1))


def solution(mesh):
    in_specs = (
        P("chan", "slab", None),
        P("chan", "slab", None),
        P("chan", "slab", None),
        P("chan", "slab", None),
        P(None, "chan", None),
        P(None, "chan", None),
    )
    out_specs = (P("chan", "slab", None), P(None, "chan", "slab"), P(None, "chan", "slab"))
    return jax.shard_map(
        per_device, mesh=mesh, in_specs=in_specs, out_specs=out_specs, check_vma=False
    )
```
